32 devices in a mesh: row: 4 (over x, core), col: 8 (over z, y).
Axes of the slice: x: 2, y: 2, z: 4, core: 2. Of those that a mesh axis runs over, the one named last changes fastest.
Arguments:
- matrix: float32 [2048, 2048], P('row', 'col'), as said below
- panel: float32 [2048, 256], P(('row', 'col')), may hold values from -0.125 to 0.125
- factor: float32 [256, 256], replicated, as said below
Outputs:
- updated: float32 [2048, 2048], P('row', 'col')
- correction: float32 [2048, 256], P(('row', 'col'))
The draws below stay inside these ranges and needn't reach their ends.
Inputs may be any that keep to these rules, and one draw needn't show every extreme that they name: `matrix`: symmetric. `factor`: upper triangular with a positive diagonal.
All inputs are finite; a program needn't handle non-finite values.
Results may differ from the reference program's by a relative error of at most 0.000071.
Values sent between devices are 32-bit elements; how exact they have to be, the bound alone decides.
A program may use at most 64 MiB of HBM per device.

```python
import math
import jax
import jax.numpy as jnp
from jax import lax

B = 256
N = 2048


def draw_matrix(key, part):
    noise = jax.random.normal(key, (N, N), jnp.float32)
    return (noise + noise.T) * 0.70710678


def draw_factor(key, part):
    upper = jax.random.normal(jax.random.fold_in(key, 3), (B, B), jnp.float32) * (0.5 / math.sqrt(B))
    diag_vals = jax.random.uniform(jax.random.fold_in(key, 5), (B,), jnp.float32, 0.6, 1.4)
    return jnp.triu(upper, 1) + jnp.diag(diag_vals)


def level_of(stream_key, dims, shards, smallest, high):
    loudness, own = 1.0, jax.random.fold_in(stream_key, 6)
    for dim, shards_of in shards:
        heights = jnp.exp(jax.random.uniform(jax.random.fold_in(own, dim), (shards_of,), jnp.float32, smallest / len(shards), high / len(shards)))
        loudness = loudness * jnp.repeat(heights, dims[dim] // shards_of).reshape([-1 if axis == dim else 1 for axis in range(len(dims))])
    return loudness


def bell_draw(rng, dims, width, limit, pieces=(), dtype=jnp.bfloat16):
    values = jax.random.normal(rng, dims, jnp.float32) * width
    if len(pieces) > 0:
        values = level_of(rng, dims, pieces, -0.22, 0.18) * values
    return jnp.clip(values, min=-limit, max=limit).astype(dtype)


def setup_inputs(seed: int = 0) -> dict:
    keys = jax.random.split(jax.random.key(seed), 4)
    return {
        "matrix": draw_matrix(jax.random.fold_in(keys[3], 71), 0),
        "panel": bell_draw(keys[1], (N, B), N ** -0.5, 0.125, ((0, 32),), jnp.float32),
        "factor": draw_factor(jax.random.fold_in(keys[3], 71), 0),
    }


def mult(left, right):
    return jnp.dot(left, right, precision=lax.Precision.HIGHEST, preferred_element_type=jnp.float32)


def reference(matrix, panel, factor):
    product = mult(matrix, panel)
    scaled = mult(product, factor)
    small = mult(panel.T, scaled)
    correction = scaled - 0.5 * mult(panel, mult(factor.T, small))
    updated = matrix - mult(panel, correction.T) - mult(correction, panel.T)
    return updated, correction
```

```python
import functools

import jax
import jax.numpy as jnp
from jax import lax
from jax.experimental import pallas as pl
from jax.experimental.pallas import tpu as pltpu
from jax.sharding import PartitionSpec as P

F32 = jnp.float32
BF16 = jnp.bfloat16
NN = (((1,), (0,)), ((), ()))
NT = (((1,), (1,)), ((), ()))


def split(x):
    high = x.astype(BF16)
    return high, (x - high.astype(F32)).astype(BF16)


def mult(a, b, dims=NN):
    dot = functools.partial(lax.dot_general, dimension_numbers=dims, preferred_element_type=F32)
    return dot(a[0], b[1]) + dot(a[1], b[0]) + dot(a[0], b[0])


def wide_of(ref, span):
    return jnp.concatenate([ref[0, span, :], ref[1, span, :]], axis=1)


def tile_loop(count, body):
    if count <= 2:
        for i in range(count):
            body(i)
    else:
        pl.loop(0, count)(body)


def kernel(nrows, ncols, tile, a_hbm, panel_hbm, t_hbm, out_ref, corr_ref,
           a_ref, t_ref, vr, vc, sr, sc, q, qin, kpart, kin, kpair, kfull, klast, klin,
           at_hi, at_lo, vt_hi, vt_lo,
           local_sem, v_send, v_recv, vf_send, vf_recv, q_send, q_recv,
           s_send, s_recv, sd_send, sf_send, sf_recv, sc_send, sc_recv,
           vc_send, vc_recv, k_send, k_recv, kg_send, kg_recv, kl_send, kl_recv):
    r, c = lax.axis_index("row"), lax.axis_index("col")
    lines = ncols // 2
    group = ncols // (2 * nrows)
    z, y = c // 2, c % 2
    total = a_ref.shape[0]
    nh, wide, hw = sc.shape
    blk, width = panel_hbm.shape
    tiles = total // tile
    half = width // 2
    mate = r + 1 - 2 * (r % 2)
    far = lines // 2

    def rows(index, size):
        return pl.ds(pl.multiple_of(index * size, size), size)

    def peer(d):
        line = z
        for b in range(lines.bit_length()):
            if d >> b & 1:
                line = line + (1 << b) - (2 << b) * (z // (1 << b) % 2)
        return line

    def copy(src, dst, send, recv, row, col):
        return pltpu.make_async_remote_copy(
            src_ref=src, dst_ref=dst, send_sem=send, recv_sem=recv,
            device_id=(row, col), device_id_type=pl.DeviceIdType.MESH)

    sends = []

    def go(desc, when=None):
        if when is None:
            desc.start()
        else:
            pl.when(when)(desc.start)
        sends.append((desc, when))

    opposite = peer(far)
    across = z * 2 + 1 - y
    target = z // group
    barrier = pltpu.get_barrier_semaphore()

    def greet(row, col):
        pl.semaphore_signal(barrier, inc=1, device_id=(row, col), device_id_type=pl.DeviceIdType.MESH)

    for d in range(1, lines):
        greet(r, peer(d) * 2 + y)
    greet(r, across)
    greet(r, opposite * 2 + 1 - y)
    for d in range(1, nrows):
        greet(lax.rem(r + d, nrows), c)
    for g in range(group):
        line = r * group + g

        @pl.when(z != line)
        def _():
            for d in range(1, nrows):
                greet(lax.rem(r + d, nrows), line * 2 + y)

        @pl.when(opposite == line)
        def _():
            for d in range(1, nrows):
                greet(lax.rem(r + d, nrows), line * 2 + 1 - y)

    loads = [pltpu.make_async_copy(panel_hbm.at[:, pl.ds(h * hw, hw)], vr.at[h, rows(c, blk), :], local_sem.at[h])
             for h in range(nh)]
    loads.append(pltpu.make_async_copy(a_hbm, a_ref, local_sem.at[nh]))
    loads.append(pltpu.make_async_copy(t_hbm, t_ref, local_sem.at[nh + 1]))
    for load in loads:
        load.start()
    for h in range(nh):
        loads[h].wait()
    pl.semaphore_wait(barrier, lines + nrows + jnp.where(target == r, 0, lines))

    order = [d for d in reversed(range(1, lines)) if d != far] + [far]
    for h in range(nh):
        own = vr.at[h, rows(c, blk), :]
        go(copy(own, own, v_send.at[h, z], v_recv.at[h, z], r, across))
        for d in order:
            go(copy(own, own, v_send.at[h, peer(d)], v_recv.at[h, z], r, peer(d) * 2 + y))
        go(copy(own, own, vf_send.at[h, opposite], vf_recv.at[h, z], r, opposite * 2 + 1 - y))

    loads[nh].wait()

    def flip(i):
        high, low = split(a_ref[pl.ds(pl.multiple_of(i * tile, tile), tile), :].T)
        at_hi[i] = high
        at_lo[i] = low
    tile_loop(tiles, flip)
    loads[nh + 1].wait()
    t_two = split(t_ref[...])
    tt_two = split(t_ref[...].T)

    def arrived(h, line, side, recv):
        slot = vr.at[h, rows(line * 2 + side, blk), :]
        copy(slot, slot, v_send.at[h, line], recv.at[h, line], r, c).wait_recv()
        return slot

    for h in range(nh):
        for d in range(1, lines):
            if d != far:
                line = peer(d)
                slot = arrived(h, line, y, v_recv)
                go(copy(slot, slot, vf_send.at[h, line], vf_recv.at[h, line], r, across))

    def reduce_product(h):
        for e in range(tiles):
            for d in (2 * e, 2 * e + 1):
                line = peer(d)
                if d == far:
                    arrived(h, line, y, v_recv)
                arrived(h, line, 1 - y, vf_recv if d else v_recv)
            i = peer(2 * e) // 2
            part = mult((at_hi[i], at_lo[i]), split(vr[h, rows(i, tile), :]))
            q[h] = part if e == 0 else q[h] + part
        for d in range(1, nrows):
            other = lax.rem(r + d, nrows)
            go(copy(q.at[h, rows(other, blk), :], qin.at[h, d], q_send.at[h, d], q_recv.at[h, d], other, c))

    for h in range(nh):
        reduce_product(h)

    def turn(i):
        span = pl.ds(pl.multiple_of(i * tile, tile), tile)
        high, low = split(mult(tt_two, split(wide_of(vr, span)), NT))
        vt_hi[i] = high
        vt_lo[i] = low
    tile_loop(tiles, turn)

    place = lax.rem(c * nrows + r, ncols)
    here = r * group + lax.rem(z, group)
    products = []
    for h in range(nh):
        for d in range(1, nrows):
            copy(qin.at[h, d], qin.at[h, d], q_send.at[h, d], q_recv.at[h, d], r, c).wait_recv()
        product = q[h, rows(r, blk), :]
        for d in range(1, nrows):
            product = product + qin[h, d]
        products.append(split(product))
        scaled = None
        for g in range(h + 1):
            block = tuple(t[g * hw:(g + 1) * hw, h * hw:(h + 1) * hw] for t in t_two)
            term = mult(products[g], block)
            scaled = term if scaled is None else scaled + term
        mine = sc.at[h, rows(r, blk), :]
        mine[...] = scaled
        slot = sr.at[h, rows(place, blk), :]
        for d in order:
            go(copy(mine, slot, s_send.at[h, peer(d)], s_recv.at[h, here], target, peer(d) * 2 + y))
        go(copy(mine, slot, sd_send.at[h], sf_recv.at[h, here], target, opposite * 2 + 1 - y))
        for d in range(1, nrows):
            go(copy(mine, mine, sc_send.at[h, d], sc_recv.at[h, d], lax.rem(r + d, nrows), c))

    holder = c * nrows // ncols
    first_block = lax.rem(c * nrows, ncols)
    v_slice = vr.at[:, rows(first_block // nrows, wide), :]
    same = r % 2 == holder % 2
    for d in range(1, nrows // 2):
        go(copy(v_slice, vc, vc_send.at[d], vc_recv.at[0], lax.rem(r + 2 * d, nrows), c), r == holder)
    to_mate = copy(v_slice, vc, vc_send.at[0], vc_recv.at[0], mate, c)

    @pl.when(r == holder)
    def _():
        to_mate.start()
        vc[...] = v_slice[...]

    def forward_scaled(h):
        for d in range(1, nrows):
            slot = sc.at[h, rows(lax.rem(r - d + nrows, nrows), blk), :]
            copy(slot, slot, sc_send.at[h, d], sc_recv.at[h, d], r, c).wait_recv()
        for g in range(group):
            line = r * group + g
            for d in range(nrows):
                j = lax.rem(r + d, nrows)
                at = j * group + g
                slot = sr.at[h, rows(lax.rem((line * 2 + y) * nrows + j, ncols), blk), :]
                held = sc.at[h, rows(j, blk), :]
                straight = copy(held, slot, sf_send.at[h, at], sf_recv.at[h, at], r, across)
                passed = copy(slot, slot, sf_send.at[h, at], sf_recv.at[h, at], r, across)
                came = copy(slot, slot, s_send.at[h, 0], s_recv.at[h, at], r, c)

                @pl.when(z == line)
                def _():
                    straight.start()
                    slot[...] = held[...]

                @pl.when(z != line)
                def _():
                    came.wait_recv()

                    @pl.when(opposite != line)
                    def _():
                        passed.start()
                sends.append((passed, opposite != line))

    def gather_scaled(h):
        for g in range(group):
            line = r * group + g
            for j in range(nrows):
                at = j * group + g
                slot = sr.at[h, rows(lax.rem((line * 2 + 1 - y) * nrows + j, ncols), blk), :]
                copy(slot, slot, sf_send.at[h, at], sf_recv.at[h, at], r, c).wait_recv()

    for h in range(nh):
        forward_scaled(h)

    gather_scaled(0)
    kpart[...] = jnp.zeros_like(kpart)

    def inner(i):
        span = pl.ds(pl.multiple_of(i * tile, tile), tile)
        kpart[...] += mult((vt_hi[i], vt_lo[i]), split(sr[0, span, :]))
    tile_loop(tiles, inner)
    go(copy(kpart.at[rows(mate % 2, half), :], kin.at[0], k_send.at[0], k_recv.at[0], mate, c))

    arrival = copy(vc, vc, vc_send.at[0], vc_recv.at[0], r, c)
    onward = copy(vc, vc, vc_send.at[0], vc_recv.at[0], mate, c)

    @pl.when(r != holder)
    def _():
        arrival.wait_recv()

        @pl.when(same)
        def _():
            onward.start()
    sends.append((onward, same))

    copy(kin.at[0], kin.at[0], k_send.at[0], k_recv.at[0], r, c).wait_recv()
    kpair[...] = kpart[rows(r % 2, half), :] + kin[0]
    for d in range(1, nrows // 2):
        go(copy(kpair, kin.at[d], k_send.at[d], k_recv.at[d], lax.rem(r + 2 * d, nrows), c))

    gather_scaled(1)
    klast[...] = jnp.zeros_like(klast)

    def inner_last(i):
        span = pl.ds(pl.multiple_of(i * tile, tile), tile)
        klast[...] += mult((vt_hi[i, hw:, :], vt_lo[i, hw:, :]), split(sr[1, span, :]))
    tile_loop(tiles, inner_last)
    for d in range(1, nrows):
        go(copy(klast, klin.at[d], kl_send.at[d], kl_recv.at[d], lax.rem(r + d, nrows), c))

    for d in range(1, nrows // 2):
        copy(kpair, kin.at[d], k_send.at[d], k_recv.at[d], r, c).wait_recv()
    summed = kpair[...]
    for d in range(1, nrows // 2):
        summed = summed + kin[d]
    mine_half = kfull.at[rows(r % 2, half), :]
    mine_half[...] = summed
    go(copy(mine_half, mine_half, kg_send.at[0], kg_recv.at[0], mate, c))

    everything = pl.ds(0, wide)
    vc_two = split(wide_of(vc, everything))

    def first(i):
        span = pl.ds(pl.multiple_of(i * tile, tile), tile)
        out_ref[span, :] = a_ref[span, :] - mult(split(wide_of(sr, span)), vc_two, NT)
    tile_loop(tiles, first)

    other_half = kfull.at[rows(mate % 2, half), :]
    copy(other_half, other_half, kg_send.at[0], kg_recv.at[0], r, c).wait_recv()
    k_two = split(kfull[...])
    k_turned = tuple(k[hw:, :] for k in k_two)
    vc_parts = [tuple(v[:, h * hw:(h + 1) * hw] for v in vc_two) for h in range(nh)]
    y_two = split(sc[0] - mult(vc_two, k_two))
    y_rest = sc[1] - mult(vc_parts[0], k_turned, NT)

    def second(i):
        span = pl.ds(pl.multiple_of(i * tile, tile), tile)
        out_ref[span, :] = out_ref[span, :] - mult(split(vr[0, span, :]), y_two, NT)
    tile_loop(tiles, second)
    mine = rows(c, blk)
    corr_ref[:, :hw] = sr[0, mine, :] - 0.5 * mult(split(wide_of(vr, mine)), k_two)
    corr_rest = mult(split(vr[0, mine, :]), k_turned, NT)

    for d in range(1, nrows):
        copy(klast, klin.at[d], kl_send.at[d], kl_recv.at[d], r, c).wait_recv()
    last = klast[...]
    for d in range(1, nrows):
        last = last + klin[d]
    last_two = split(last)
    y_last = split(y_rest - mult(vc_parts[1], last_two))

    def third(i):
        span = pl.ds(pl.multiple_of(i * tile, tile), tile)
        out_ref[span, :] = out_ref[span, :] - mult(split(vr[1, span, :]), y_last, NT)
    tile_loop(tiles, third)
    corr_ref[:, hw:] = sr[1, mine, :] - 0.5 * (corr_rest + mult(split(vr[1, mine, :]), last_two))

    pl.when(r == holder)(to_mate.wait_send)
    for desc, when in sends:
        if when is None:
            desc.wait_send()
        elif desc is onward:
            pl.when((r != holder) & when)(desc.wait_send)
        else:
            pl.when(when)(desc.wait_send)


def hand_out(held_ref, held_corr_ref, out_ref, corr_ref):
    out_ref[...] = held_ref[...]
    corr_ref[...] = held_corr_ref[...]


def per_device(nrows, ncols, matrix, panel, factor):
    total, wide = matrix.shape
    blk, width = panel.shape
    tile = 4 * blk
    tiles = total // tile
    group = ncols // (2 * nrows)
    lines = ncols // 2
    nh = 2
    hw = width // nh
    dma = pltpu.SemaphoreType.DMA
    vmem = pl.BlockSpec(memory_space=pltpu.VMEM)
    hbm = pl.BlockSpec(memory_space=pltpu.HBM)
    limit = 4 * (5 * total * wide + 4 * total * width + 4 * wide * width + 16 * width * width) + (8 << 20)
    held = pl.pallas_call(
        functools.partial(kernel, nrows, ncols, tile),
        out_shape=(jax.ShapeDtypeStruct(matrix.shape, F32), jax.ShapeDtypeStruct(panel.shape, F32)),
        in_specs=[hbm] * 3,
        out_specs=(vmem, vmem),
        scratch_shapes=[
            pltpu.VMEM((total, wide), F32),
            pltpu.VMEM((width, width), F32),
            pltpu.VMEM((nh, total, hw), F32),
            pltpu.VMEM((nh, wide, hw), F32),
            pltpu.VMEM((nh, total, hw), F32),
            pltpu.VMEM((nh, wide, hw), F32),
            pltpu.VMEM((nh, wide, hw), F32),
            pltpu.VMEM((nh, nrows, blk, hw), F32),
            pltpu.VMEM((width, hw), F32),
            pltpu.VMEM((nrows // 2, width // 2, hw), F32),
            pltpu.VMEM((width // 2, hw), F32),
            pltpu.VMEM((width, hw), F32),
            pltpu.VMEM((hw, hw), F32),
            pltpu.VMEM((nrows, hw, hw), F32),
            pltpu.VMEM((tiles, wide, tile), BF16),
            pltpu.VMEM((tiles, wide, tile), BF16),
            pltpu.VMEM((tiles, width, tile), BF16),
            pltpu.VMEM((tiles, width, tile), BF16),
            dma((nh + 2,)),
            dma((nh, lines)), dma((nh, lines)), dma((nh, lines)), dma((nh, lines)),
            dma((nh, nrows)), dma((nh, nrows)),
            dma((nh, lines)), dma((nh, nrows * group)), dma((nh,)),
            dma((nh, nrows * group)), dma((nh, nrows * group)),
            dma((nh, nrows)), dma((nh, nrows)),
            dma((nrows,)), dma((1,)), dma((nrows,)), dma((nrows,)), dma((1,)), dma((1,)),
            dma((nrows,)), dma((nrows,)),
        ],
        compiler_params=pltpu.CompilerParams(
            collective_id=0, has_side_effects=True, vmem_limit_bytes=limit),
    )(matrix, panel, factor)
    return pl.pallas_call(
        hand_out,
        out_shape=(jax.ShapeDtypeStruct(matrix.shape, F32), jax.ShapeDtypeStruct(panel.shape, F32)),
        in_specs=[vmem] * 2,
        out_specs=(vmem, vmem),
        compiler_params=pltpu.CompilerParams(vmem_limit_bytes=6 * total * wide * 4 + (1 << 20)),
    )(*held)


def solution(mesh):
    in_specs = (P("row", "col"), P(("row", "col"), None), P())
    out_specs = (P("row", "col"), P(("row", "col"), None))
    return jax.shard_map(
        functools.partial(per_device, mesh.shape["row"], mesh.shape["col"]),
        mesh=mesh, in_specs=in_specs, out_specs=out_specs, check_vma=False)
```

```python
import functools

import jax
import jax.numpy as jnp
from jax import lax
from jax.experimental import pallas as pl
from jax.experimental.pallas import tpu as pltpu
from jax.sharding import PartitionSpec as P

F32 = jnp.float32
BF16 = jnp.bfloat16
NN = (((1,), (0,)), ((), ()))
NT = (((1,), (1,)), ((), ()))


def split(x):
    high = x.astype(BF16)
    return high, (x - high.astype(F32)).astype(BF16)


def mult(a, b, dims=NN):
    dot = functools.partial(lax.dot_general, dimension_numbers=dims, preferred_element_type=F32)
    return dot(a[0], b[1]) + dot(a[1], b[0]) + dot(a[0], b[0])


def wide_of(ref, span):
    return jnp.concatenate([ref[0, span, :], ref[1, span, :]], axis=1)


def tile_loop(count, body):
    if count <= 2:
        for i in range(count):
            body(i)
    else:
        pl.loop(0, count)(body)


def kernel(nrows, ncols, tile, a_hbm, panel_hbm, t_hbm, out_ref, corr_ref,
           a_ref, t_ref, vr, vc, sr, sc, q, qin, kpart, kin, kpair, kfull, klast, klin,
           at_hi, at_lo, vt_hi, vt_lo,
           local_sem, v_send, v_recv, vf_send, vf_recv, q_send, q_recv,
           s_send, s_recv, sd_send, sf_send, sf_recv, sc_send, sc_recv,
           vc_send, vc_recv, k_send, k_recv, kg_send, kg_recv, kl_send, kl_recv):
    r, c = lax.axis_index("row"), lax.axis_index("col")
    lines = ncols // 2
    group = ncols // (2 * nrows)
    z, y = c // 2, c % 2
    total = a_ref.shape[0]
    nh, wide, hw = sc.shape
    blk, width = panel_hbm.shape
    tiles = total // tile
    half = width // 2
    mate = r + 1 - 2 * (r % 2)
    far = lines // 2

    def rows(index, size):
        return pl.ds(pl.multiple_of(index * size, size), size)

    def peer(d):
        line = z
        for b in range(lines.bit_length()):
            if d >> b & 1:
                line = line + (1 << b) - (2 << b) * (z // (1 << b) % 2)
        return line

    def copy(src, dst, send, recv, row, col):
        return pltpu.make_async_remote_copy(
            src_ref=src, dst_ref=dst, send_sem=send, recv_sem=recv,
            device_id=(row, col), device_id_type=pl.DeviceIdType.MESH)

    sends = []

    def go(desc, when=None):
        if when is None:
            desc.start()
        else:
            pl.when(when)(desc.start)
        sends.append((desc, when))

    opposite = peer(far)
    across = z * 2 + 1 - y
    target = z // group
    barrier = pltpu.get_barrier_semaphore()

    def greet(row, col):
        pl.semaphore_signal(barrier, inc=1, device_id=(row, col), device_id_type=pl.DeviceIdType.MESH)

    for d in range(1, lines):
        greet(r, peer(d) * 2 + y)
    greet(r, across)
    greet(r, opposite * 2 + 1 - y)
    for d in range(1, nrows):
        greet(lax.rem(r + d, nrows), c)
    for g in range(group):
        line = r * group + g

        @pl.when(z != line)
        def _():
            for d in range(1, nrows):
                greet(lax.rem(r + d, nrows), line * 2 + y)

        @pl.when(opposite == line)
        def _():
            for d in range(1, nrows):
                greet(lax.rem(r + d, nrows), line * 2 + 1 - y)

    loads = [pltpu.make_async_copy(panel_hbm.at[:, pl.ds(h * hw, hw)], vr.at[h, rows(c, blk), :], local_sem.at[h])
             for h in range(nh)]
    loads.append(pltpu.make_async_copy(a_hbm, a_ref, local_sem.at[nh]))
    loads.append(pltpu.make_async_copy(t_hbm, t_ref, local_sem.at[nh + 1]))
    for load in loads:
        load.start()
    for h in range(nh):
        loads[h].wait()
    pl.semaphore_wait(barrier, lines + nrows + jnp.where(target == r, 0, lines))

    order = [d for d in reversed(range(1, lines)) if d != far] + [far]
    for h in range(nh):
        own = vr.at[h, rows(c, blk), :]
        go(copy(own, own, v_send.at[h, z], v_recv.at[h, z], r, across))
        for d in order:
            go(copy(own, own, v_send.at[h, peer(d)], v_recv.at[h, z], r, peer(d) * 2 + y))
        go(copy(own, own, vf_send.at[h, opposite], vf_recv.at[h, z], r, opposite * 2 + 1 - y))

    loads[nh].wait()

    def flip(i):
        high, low = split(a_ref[pl.ds(pl.multiple_of(i * tile, tile), tile), :].T)
        at_hi[i] = high
        at_lo[i] = low
    tile_loop(tiles, flip)
    loads[nh + 1].wait()
    t_two = split(t_ref[...])
    tt_two = split(t_ref[...].T)

    def arrived(h, line, side, recv):
        slot = vr.at[h, rows(line * 2 + side, blk), :]
        copy(slot, slot, v_send.at[h, line], recv.at[h, line], r, c).wait_recv()
        return slot

    for h in range(nh):
        for d in range(1, lines):
            if d != far:
                line = peer(d)
                slot = arrived(h, line, y, v_recv)
                go(copy(slot, slot, vf_send.at[h, line], vf_recv.at[h, line], r, across))

    def reduce_product(h):
        for e in range(tiles):
            for d in (2 * e, 2 * e + 1):
                line = peer(d)
                if d == far:
                    arrived(h, line, y, v_recv)
                arrived(h, line, 1 - y, vf_recv if d else v_recv)
            i = peer(2 * e) // 2
            part = mult((at_hi[i], at_lo[i]), split(vr[h, rows(i, tile), :]))
            q[h] = part if e == 0 else q[h] + part
        for d in range(1, nrows):
            other = lax.rem(r + d, nrows)
            go(copy(q.at[h, rows(other, blk), :], qin.at[h, d], q_send.at[h, d], q_recv.at[h, d], other, c))

    for h in range(nh):
        reduce_product(h)

    def turn(i):
        span = pl.ds(pl.multiple_of(i * tile, tile), tile)
        high, low = split(mult(tt_two, split(wide_of(vr, span)), NT))
        vt_hi[i] = high
        vt_lo[i] = low
    tile_loop(tiles, turn)

    place = lax.rem(c * nrows + r, ncols)
    here = r * group + lax.rem(z, group)
    products = []
    for h in range(nh):
        for d in range(1, nrows):
            copy(qin.at[h, d], qin.at[h, d], q_send.at[h, d], q_recv.at[h, d], r, c).wait_recv()
        product = q[h, rows(r, blk), :]
        for d in range(1, nrows):
            product = product + qin[h, d]
        products.append(split(product))
        scaled = None
        for g in range(h + 1):
            block = tuple(t[g * hw:(g + 1) * hw, h * hw:(h + 1) * hw] for t in t_two)
            term = mult(products[g], block)
            scaled = term if scaled is None else scaled + term
        mine = sc.at[h, rows(r, blk), :]
        mine[...] = scaled
        slot = sr.at[h, rows(place, blk), :]
        for d in order:
            go(copy(mine, slot, s_send.at[h, peer(d)], s_recv.at[h, here], target, peer(d) * 2 + y))
        go(copy(mine, slot, sd_send.at[h], sf_recv.at[h, here], target, opposite * 2 + 1 - y))
        for d in range(1, nrows):
            go(copy(mine, mine, sc_send.at[h, d], sc_recv.at[h, d], lax.rem(r + d, nrows), c))

    holder = c * nrows // ncols
    first_block = lax.rem(c * nrows, ncols)
    v_slice = vr.at[:, rows(first_block // nrows, wide), :]
    same = r % 2 == holder % 2
    for d in range(1, nrows // 2):
        go(copy(v_slice, vc, vc_send.at[d], vc_recv.at[0], lax.rem(r + 2 * d, nrows), c), r == holder)
    to_mate = copy(v_slice, vc, vc_send.at[0], vc_recv.at[0], mate, c)

    @pl.when(r == holder)
    def _():
        to_mate.start()
        vc[...] = v_slice[...]

    def forward_scaled(h):
        for d in range(1, nrows):
            slot = sc.at[h, rows(lax.rem(r - d + nrows, nrows), blk), :]
            copy(slot, slot, sc_send.at[h, d], sc_recv.at[h, d], r, c).wait_recv()
        for g in range(group):
            line = r * group + g
            for d in range(nrows):
                j = lax.rem(r + d, nrows)
                at = j * group + g
                slot = sr.at[h, rows(lax.rem((line * 2 + y) * nrows + j, ncols), blk), :]
                held = sc.at[h, rows(j, blk), :]
                straight = copy(held, slot, sf_send.at[h, at], sf_recv.at[h, at], r, across)
                passed = copy(slot, slot, sf_send.at[h, at], sf_recv.at[h, at], r, across)
                came = copy(slot, slot, s_send.at[h, 0], s_recv.at[h, at], r, c)

                @pl.when(z == line)
                def _():
                    straight.start()
                    slot[...] = held[...]

                @pl.when(z != line)
                def _():
                    came.wait_recv()

                    @pl.when(opposite != line)
                    def _():
                        passed.start()
                sends.append((passed, opposite != line))

    def gather_scaled(h):
        for g in range(group):
            line = r * group + g
            for j in range(nrows):
                at = j * group + g
                slot = sr.at[h, rows(lax.rem((line * 2 + 1 - y) * nrows + j, ncols), blk), :]
                copy(slot, slot, sf_send.at[h, at], sf_recv.at[h, at], r, c).wait_recv()

    for h in range(nh):
        forward_scaled(h)

    gather_scaled(0)
    kpart[...] = jnp.zeros_like(kpart)

    def inner(i):
        span = pl.ds(pl.multiple_of(i * tile, tile), tile)
        kpart[...] += mult((vt_hi[i], vt_lo[i]), split(sr[0, span, :]))
    tile_loop(tiles, inner)
    go(copy(kpart.at[rows(mate % 2, half), :], kin.at[0], k_send.at[0], k_recv.at[0], mate, c))

    arrival = copy(vc, vc, vc_send.at[0], vc_recv.at[0], r, c)
    onward = copy(vc, vc, vc_send.at[0], vc_recv.at[0], mate, c)

    @pl.when(r != holder)
    def _():
        arrival.wait_recv()

        @pl.when(same)
        def _():
            onward.start()
    sends.append((onward, same))

    copy(kin.at[0], kin.at[0], k_send.at[0], k_recv.at[0], r, c).wait_recv()
    kpair[...] = kpart[rows(r % 2, half), :] + kin[0]
    for d in range(1, nrows // 2):
        go(copy(kpair, kin.at[d], k_send.at[d], k_recv.at[d], lax.rem(r + 2 * d, nrows), c))

    gather_scaled(1)
    klast[...] = jnp.zeros_like(klast)

    def inner_last(i):
        span = pl.ds(pl.multiple_of(i * tile, tile), tile)
        klast[...] += mult((vt_hi[i, hw:, :], vt_lo[i, hw:, :]), split(sr[1, span, :]))
    tile_loop(tiles, inner_last)
    for d in range(1, nrows):
        go(copy(klast, klin.at[d], kl_send.at[d], kl_recv.at[d], lax.rem(r + d, nrows), c))

    for d in range(1, nrows // 2):
        copy(kpair, kin.at[d], k_send.at[d], k_recv.at[d], r, c).wait_recv()
    summed = kpair[...]
    for d in range(1, nrows // 2):
        summed = summed + kin[d]
    mine_half = kfull.at[rows(r % 2, half), :]
    mine_half[...] = summed
    go(copy(mine_half, mine_half, kg_send.at[0], kg_recv.at[0], mate, c))

    everything = pl.ds(0, wide)
    vc_two = split(wide_of(vc, everything))

    def first(i):
        span = pl.ds(pl.multiple_of(i * tile, tile), tile)
        out_ref[span, :] = a_ref[span, :] - mult(split(wide_of(sr, span)), vc_two, NT)
    tile_loop(tiles, first)

    other_half = kfull.at[rows(mate % 2, half), :]
    copy(other_half, other_half, kg_send.at[0], kg_recv.at[0], r, c).wait_recv()
    k_two = split(kfull[...])
    k_turned = tuple(k[hw:, :] for k in k_two)
    vc_parts = [tuple(v[:, h * hw:(h + 1) * hw] for v in vc_two) for h in range(nh)]
    y_two = split(sc[0] - mult(vc_two, k_two))
    y_rest = sc[1] - mult(vc_parts[0], k_turned, NT)

    def second(i):
        span = pl.ds(pl.multiple_of(i * tile, tile), tile)
        out_ref[span, :] = out_ref[span, :] - mult(split(vr[0, span, :]), y_two, NT)
    tile_loop(tiles, second)
    mine = rows(c, blk)
    corr_ref[:, :hw] = sr[0, mine, :] - 0.5 * mult(split(wide_of(vr, mine)), k_two)
    corr_rest = mult(split(vr[0, mine, :]), k_turned, NT)

    for d in range(1, nrows):
        copy(klast, klin.at[d], kl_send.at[d], kl_recv.at[d], r, c).wait_recv()
    last = klast[...]
    for d in range(1, nrows):
        last = last + klin[d]
    last_two = split(last)
    y_last = split(y_rest - mult(vc_parts[1], last_two))

    def third(i):
        span = pl.ds(pl.multiple_of(i * tile, tile), tile)
        out_ref[span, :] = out_ref[span, :] - mult(split(vr[1, span, :]), y_last, NT)
    tile_loop(tiles, third)
    corr_ref[:, hw:] = sr[1, mine, :] - 0.5 * (corr_rest + mult(split(vr[1, mine, :]), last_two))

    pl.when(r == holder)(to_mate.wait_send)
    for desc, when in sends:
        if when is None:
            desc.wait_send()
        elif desc is onward:
            pl.when((r != holder) & when)(desc.wait_send)
        else:
            pl.when(when)(desc.wait_send)


def hand_out(held_ref, held_corr_ref, out_ref, corr_ref):
    out_ref[...] = held_ref[...]
    corr_ref[...] = held_corr_ref[...]


def per_device(nrows, ncols, matrix, panel, factor):
    total, wide = matrix.shape
    blk, width = panel.shape
    tile = 4 * blk
    tiles = total // tile
    group = ncols // (2 * nrows)
    lines = ncols // 2
    nh = 2
    hw = width // nh
    dma = pltpu.SemaphoreType.DMA
    vmem = pl.BlockSpec(memory_space=pltpu.VMEM)
    hbm = pl.BlockSpec(memory_space=pltpu.HBM)
    limit = 4 * (5 * total * wide + 4 * total * width + 4 * wide * width + 16 * width * width) + (8 << 20)
    held = pl.pallas_call(
        functools.partial(kernel, nrows, ncols, tile),
        out_shape=(jax.ShapeDtypeStruct(matrix.shape, F32), jax.ShapeDtypeStruct(panel.shape, F32)),
        in_specs=[hbm] * 3,
        out_specs=(vmem, vmem),
        scratch_shapes=[
            pltpu.VMEM((total, wide), F32),
            pltpu.VMEM((width, width), F32),
            pltpu.VMEM((nh, total, hw), F32),
            pltpu.VMEM((nh, wide, hw), F32),
            pltpu.VMEM((nh, total, hw), F32),
            pltpu.VMEM((nh, wide, hw), F32),
            pltpu.VMEM((nh, wide, hw), F32),
            pltpu.VMEM((nh, nrows, blk, hw), F32),
            pltpu.VMEM((width, hw), F32),
            pltpu.VMEM((nrows // 2, width // 2, hw), F32),
            pltpu.VMEM((width // 2, hw), F32),
            pltpu.VMEM((width, hw), F32),
            pltpu.VMEM((hw, hw), F32),
            pltpu.VMEM((nrows, hw, hw), F32),
            pltpu.VMEM((tiles, wide, tile), BF16),
            pltpu.VMEM((tiles, wide, tile), BF16),
            pltpu.VMEM((tiles, width, tile), BF16),
            pltpu.VMEM((tiles, width, tile), BF16),
            dma((nh + 2,)),
            dma((nh, lines)), dma((nh, lines)), dma((nh, lines)), dma((nh, lines)),
            dma((nh, nrows)), dma((nh, nrows)),
            dma((nh, lines)), dma((nh, nrows * group)), dma((nh,)),
            dma((nh, nrows * group)), dma((nh, nrows * group)),
            dma((nh, nrows)), dma((nh, nrows)),
            dma((nrows,)), dma((1,)), dma((nrows,)), dma((nrows,)), dma((1,)), dma((1,)),
            dma((nrows,)), dma((nrows,)),
        ],
        compiler_params=pltpu.CompilerParams(
            collective_id=0, has_side_effects=True, vmem_limit_bytes=limit),
    )(*(pltpu.with_memory_space_constraint(v, pltpu.HBM) for v in (matrix, panel, factor)))
    return pl.pallas_call(
        hand_out,
        out_shape=(jax.ShapeDtypeStruct(matrix.shape, F32), jax.ShapeDtypeStruct(panel.shape, F32)),
        in_specs=[vmem] * 2,
        out_specs=(vmem, vmem),
        compiler_params=pltpu.CompilerParams(vmem_limit_bytes=6 * total * wide * 4 + (1 << 20)),
    )(*held)


def solution(mesh):
    in_specs = (P("row", "col"), P(("row", "col"), None), P())
    out_specs = (P("row", "col"), P(("row", "col"), None))
    return jax.shard_map(
        functools.partial(per_device, mesh.shape["row"], mesh.shape["col"]),
        mesh=mesh, in_specs=in_specs, out_specs=out_specs, check_vma=False)
```

```python
import functools

import jax
import jax.numpy as jnp
from jax import lax
from jax.experimental import pallas as pl
from jax.experimental.pallas import tpu as pltpu
from jax.sharding import PartitionSpec as P

F32 = jnp.float32
BF16 = jnp.bfloat16
NN = (((1,), (0,)), ((), ()))
NT = (((1,), (1,)), ((), ()))


def split(x):
    high = x.astype(BF16)
    return high, (x - high.astype(F32)).astype(BF16)


def mult(a, b, dims=NN):
    dot = functools.partial(lax.dot_general, dimension_numbers=dims, preferred_element_type=F32)
    return dot(a[0], b[1]) + dot(a[1], b[0]) + dot(a[0], b[0])


def wide_of(ref, span):
    return jnp.concatenate([ref[0, span, :], ref[1, span, :]], axis=1)


def tile_loop(count, body):
    if count <= 2:
        for i in range(count):
            body(i)
    else:
        pl.loop(0, count)(body)


def kernel(nrows, ncols, tile, a_hbm, panel_hbm, t_hbm, out_ref, corr_ref,
           a_ref, t_ref, vr, vc, sr, sc, q, qin, kpart, kin, kpair, kside, kfull,
           lpart, lin, lpair, lfull,
           at_hi, at_lo, vt_hi, vt_lo,
           local_sem, v_send, v_recv, vf_send, vf_recv, q_send, q_recv,
           s_send, s_recv, sf_send, sf_recv, sc_send, sc_recv,
           vc_send, vc_recv, k_send, k_recv, kg_send, kg_recv):
    r, c = lax.axis_index("row"), lax.axis_index("col")
    lines = ncols // 2
    group = ncols // (2 * nrows)
    z, y = c // 2, c % 2
    total = a_ref.shape[0]
    nh, wide, hw = sc.shape
    blk, width = panel_hbm.shape
    tiles = total // tile
    mate = r + 1 - 2 * (r % 2)
    far = lines // 2

    def rows(index, size):
        return pl.ds(pl.multiple_of(index * size, size), size)

    def peer(d):
        line = z
        for b in range(lines.bit_length()):
            if d >> b & 1:
                line = line + (1 << b) - (2 << b) * (z // (1 << b) % 2)
        return line

    def copy(src, dst, send, recv, row, col):
        return pltpu.make_async_remote_copy(
            src_ref=src, dst_ref=dst, send_sem=send, recv_sem=recv,
            device_id=(row, col), device_id_type=pl.DeviceIdType.MESH)

    sends = []

    def go(desc, when=None):
        if when is None:
            desc.start()
        else:
            pl.when(when)(desc.start)
        sends.append((desc, when))

    loads = [pltpu.make_async_copy(panel_hbm.at[:, pl.ds(h * hw, hw)], vr.at[h, rows(c, blk), :], local_sem.at[h])
             for h in range(nh)]
    loads.append(pltpu.make_async_copy(a_hbm, a_ref, local_sem.at[nh]))
    loads.append(pltpu.make_async_copy(t_hbm, t_ref, local_sem.at[nh + 1]))
    for load in loads:
        load.start()

    opposite = peer(far)
    across = z * 2 + 1 - y
    target = z // group
    barrier = pltpu.get_barrier_semaphore()

    def greet(row, col):
        pl.semaphore_signal(barrier, inc=1, device_id=(row, col), device_id_type=pl.DeviceIdType.MESH)

    for d in range(1, lines):
        greet(r, peer(d) * 2 + y)
    greet(r, across)
    greet(r, opposite * 2 + 1 - y)
    for d in range(1, nrows):
        greet(lax.rem(r + d, nrows), c)
    for d in range(1, nrows // 2):
        greet(lax.rem(r + 2 * d, nrows), across)
    for g in range(group):
        line = r * group + g

        @pl.when(z != line)
        def _():
            for d in range(1, nrows):
                greet(lax.rem(r + d, nrows), line * 2 + y)

    for h in range(nh):
        loads[h].wait()
    pl.semaphore_wait(barrier, lines + nrows + nrows // 2 - 1 + jnp.where(target == r, 0, lines - 1))

    crossing = (False, False)
    order = [d for d in reversed(range(1, lines)) if d != far] + [far]
    for h in range(nh):
        own = vr.at[h, rows(c, blk), :]
        go(copy(own, own, v_send.at[h, z], v_recv.at[h, z], r, across))
        for d in order:
            go(copy(own, own, v_send.at[h, peer(d)], v_recv.at[h, z], r, peer(d) * 2 + y))
        if crossing[h]:
            go(copy(own, own, vf_send.at[h, opposite], vf_recv.at[h, z], r, opposite * 2 + 1 - y))

    loads[nh].wait()

    def flip(i):
        high, low = split(a_ref[pl.ds(pl.multiple_of(i * tile, tile), tile), :].T)
        at_hi[i] = high
        at_lo[i] = low
    tile_loop(tiles, flip)
    loads[nh + 1].wait()
    t_two = split(t_ref[...])
    tt_two = split(t_ref[...].T)

    def arrived(h, line, side, recv):
        slot = vr.at[h, rows(line * 2 + side, blk), :]
        copy(slot, slot, v_send.at[h, line], recv.at[h, line], r, c).wait_recv()
        return slot

    for h in range(nh):
        for d in sorted(range(1, lines), key=lambda d: d == far):
            if d != far or not crossing[h]:
                line = peer(d)
                slot = arrived(h, line, y, v_recv)
                go(copy(slot, slot, vf_send.at[h, line], vf_recv.at[h, line], r, across))

    def reduce_product(h):
        for e in range(tiles):
            for d in (2 * e, 2 * e + 1):
                line = peer(d)
                if d == far and crossing[h]:
                    arrived(h, line, y, v_recv)
                arrived(h, line, 1 - y, vf_recv if d else v_recv)
            i = peer(2 * e) // 2
            part = mult((at_hi[i], at_lo[i]), split(vr[h, rows(i, tile), :]))
            q[h] = part if e == 0 else q[h] + part
        for d in range(1, nrows):
            other = lax.rem(r + d, nrows)
            go(copy(q.at[h, rows(other, blk), :], qin.at[h, d], q_send.at[h, d], q_recv.at[h, d], other, c))

    for h in range(nh):
        reduce_product(h)

    def turn(i):
        span = pl.ds(pl.multiple_of(i * tile, tile), tile)
        high, low = split(mult(tt_two, split(wide_of(vr, span)), NT))
        vt_hi[i] = high
        vt_lo[i] = low
    tile_loop(tiles, turn)

    place = lax.rem(c * nrows + r, ncols)
    here = r * group + lax.rem(z, group)
    products = []
    for h in range(nh):
        for d in range(1, nrows):
            copy(qin.at[h, d], qin.at[h, d], q_send.at[h, d], q_recv.at[h, d], r, c).wait_recv()
        product = q[h, rows(r, blk), :]
        for d in range(1, nrows):
            product = product + qin[h, d]
        products.append(split(product))
        scaled = None
        for g in range(h + 1):
            block = tuple(t[g * hw:(g + 1) * hw, h * hw:(h + 1) * hw] for t in t_two)
            term = mult(products[g], block)
            scaled = term if scaled is None else scaled + term
        mine = sc.at[h, rows(r, blk), :]
        mine[...] = scaled
        slot = sr.at[h, rows(place, blk), :]
        for d in order:
            go(copy(mine, slot, s_send.at[h, peer(d)], s_recv.at[h, here], target, peer(d) * 2 + y))
        for d in range(1, nrows // 2):
            go(copy(mine, mine, sc_send.at[h, 2 * d], sc_recv.at[h, 2 * d], lax.rem(r + 2 * d, nrows), c))
        go(copy(mine, mine, sc_send.at[h, 1], sc_recv.at[h, 1], mate, c))

    holder = c * nrows // ncols
    first_block = lax.rem(c * nrows, ncols)
    v_slice = vr.at[:, rows(first_block // nrows, wide), :]
    same = r % 2 == holder % 2
    def from_mate(h):
        for d in range(nrows // 2):
            slot = sc.at[h, rows(lax.rem(mate - 2 * d + nrows, nrows), blk), :]
            copy(slot, slot, sc_send.at[h, 2 * d + 1], sc_recv.at[h, 2 * d + 1], r, c).wait_recv()

    def forward_scaled(h):
        for d in range(1, nrows // 2):
            slot = sc.at[h, rows(lax.rem(r - 2 * d + nrows, nrows), blk), :]
            copy(slot, slot, sc_send.at[h, 2 * d], sc_recv.at[h, 2 * d], r, c).wait_recv()
            go(copy(slot, slot, sc_send.at[h, 2 * d + 1], sc_recv.at[h, 2 * d + 1], mate, c))
        pl.when(target == r)(functools.partial(from_mate, h))
        for g in range(group):
            line = r * group + g
            for d in range(nrows):
                j = lax.rem(r + d, nrows)
                at = j * group + g
                slot = sr.at[h, rows(lax.rem((line * 2 + y) * nrows + j, ncols), blk), :]
                held = sc.at[h, rows(j, blk), :]
                straight = copy(held, slot, sf_send.at[h, at], sf_recv.at[h, at], r, across)
                passed = copy(slot, slot, sf_send.at[h, at], sf_recv.at[h, at], r, across)
                came = copy(slot, slot, s_send.at[h, 0], s_recv.at[h, at], r, c)

                @pl.when(z == line)
                def _():
                    straight.start()
                    slot[...] = held[...]

                @pl.when(z != line)
                def _():
                    came.wait_recv()
                    passed.start()
                sends.append((passed, None))

    def gather_scaled(h):
        for g in range(group):
            line = r * group + g
            for j in range(nrows):
                at = j * group + g
                slot = sr.at[h, rows(lax.rem((line * 2 + 1 - y) * nrows + j, ncols), blk), :]
                copy(slot, slot, sf_send.at[h, at], sf_recv.at[h, at], r, c).wait_recv()

    def small(h, part, base):
        part[...] = jnp.zeros_like(part)
        for g in range(group):
            start = lax.rem(((r * group + g) * 2 + y) * nrows, ncols) * blk // tile
            for i in range(nrows * blk // tile):
                at = start + i
                part[...] += mult((vt_hi[at, base:, :], vt_lo[at, base:, :]), split(sr[h, rows(at, tile), :]))

    def pair_up(h, part, room, pair):
        size = pair.shape[0]
        go(copy(part.at[rows(mate % 2, size), :], room.at[0], k_send.at[h, 0], k_recv.at[h, 0], mate, c))
        copy(room.at[0], room.at[0], k_send.at[h, 0], k_recv.at[h, 0], r, c).wait_recv()
        pair[...] = part[rows(r % 2, size), :] + room[0]

    def spread(h, room, pair, slots):
        for i in slots:
            row, col = lax.rem(r + i // 2 * 2, nrows), across if i % 2 else c
            go(copy(pair, room.at[i], k_send.at[h, i], k_recv.at[h, i], row, col))

    def collect(h, room, pair, slots):
        for i in slots:
            copy(pair, room.at[i], k_send.at[h, i], k_recv.at[h, i], r, c).wait_recv()
        summed = pair[...]
        for i in slots:
            summed = summed + room[i]
        return summed

    def finish_half(h, full, summed):
        mine = full.at[rows(r % 2, summed.shape[0]), :]
        mine[...] = summed
        go(copy(mine, mine, kg_send.at[h], kg_recv.at[h], mate, c))

    def completed(h, pair, full):
        other = full.at[rows(mate % 2, pair.shape[0]), :]
        copy(other, other, kg_send.at[h], kg_recv.at[h], r, c).wait_recv()
        return split(full[...])

    forward_scaled(0)
    small(0, kpart, 0)
    pair_up(0, kpart, kin, kpair)
    spread(0, kin, kpair, range(2, nrows, 2))
    forward_scaled(1)
    small(1, lpart, hw)
    pair_up(1, lpart, lin, lpair)
    spread(1, lin, lpair, range(1, nrows))
    for d in range(1, nrows // 2):
        go(copy(v_slice, vc, vc_send.at[d], vc_recv.at[0], lax.rem(r + 2 * d, nrows), c), r == holder)
    to_mate = copy(v_slice, vc, vc_send.at[0], vc_recv.at[0], mate, c)

    @pl.when(r == holder)
    def _():
        to_mate.start()
        vc[...] = v_slice[...]


    gather_scaled(0)
    kside[...] = collect(0, kin, kpair, range(2, nrows, 2))
    spread(0, kin, kside, (1,))

    arrival = copy(vc, vc, vc_send.at[0], vc_recv.at[0], r, c)
    onward = copy(vc, vc, vc_send.at[0], vc_recv.at[0], mate, c)

    @pl.when(r != holder)
    def _():
        arrival.wait_recv()

        @pl.when(same)
        def _():
            onward.start()
    sends.append((onward, same))
    gather_scaled(1)

    everything = pl.ds(0, wide)
    vc_two = split(wide_of(vc, everything))

    def first(i):
        span = pl.ds(pl.multiple_of(i * tile, tile), tile)
        out_ref[span, :] = a_ref[span, :] - mult(split(wide_of(sr, span)), vc_two, NT)
    tile_loop(tiles, first)

    finish_half(1, lfull, collect(1, lin, lpair, range(1, nrows)))
    finish_half(0, kfull, collect(0, kin, kside, (1,)))
    k_two = completed(0, kpair, kfull)
    k_turned = tuple(k[hw:, :] for k in k_two)
    vc_parts = [tuple(v[:, h * hw:(h + 1) * hw] for v in vc_two) for h in range(nh)]
    for h in range(nh):
        pl.when(target != r)(functools.partial(from_mate, h))
    y_two = split(sc[0] - mult(vc_two, k_two))
    y_rest = sc[1] - mult(vc_parts[0], k_turned, NT)

    def second(i):
        span = pl.ds(pl.multiple_of(i * tile, tile), tile)
        out_ref[span, :] = out_ref[span, :] - mult(split(vr[0, span, :]), y_two, NT)
    tile_loop(tiles, second)
    mine = rows(c, blk)
    corr_ref[:, :hw] = sr[0, mine, :] - 0.5 * mult(split(wide_of(vr, mine)), k_two)
    corr_rest = mult(split(vr[0, mine, :]), k_turned, NT)

    last_two = completed(1, lpair, lfull)
    y_last = split(y_rest - mult(vc_parts[1], last_two))

    def third(i):
        span = pl.ds(pl.multiple_of(i * tile, tile), tile)
        out_ref[span, :] = out_ref[span, :] - mult(split(vr[1, span, :]), y_last, NT)
    tile_loop(tiles, third)
    corr_ref[:, hw:] = sr[1, mine, :] - 0.5 * (corr_rest + mult(split(vr[1, mine, :]), last_two))

    pl.when(r == holder)(to_mate.wait_send)
    for desc, when in sends:
        if when is None:
            desc.wait_send()
        elif desc is onward:
            pl.when((r != holder) & when)(desc.wait_send)
        else:
            pl.when(when)(desc.wait_send)


def hand_out(held_ref, held_corr_ref, out_ref, corr_ref):
    out_ref[...] = held_ref[...]
    corr_ref[...] = held_corr_ref[...]


def per_device(nrows, ncols, matrix, panel, factor):
    total, wide = matrix.shape
    blk, width = panel.shape
    tile = 4 * blk
    tiles = total // tile
    group = ncols // (2 * nrows)
    lines = ncols // 2
    nh = 2
    hw = width // nh
    dma = pltpu.SemaphoreType.DMA
    vmem = pl.BlockSpec(memory_space=pltpu.VMEM)
    hbm = pl.BlockSpec(memory_space=pltpu.HBM)
    limit = 4 * (5 * total * wide + 4 * total * width + 4 * wide * width + 16 * width * width) + (8 << 20)
    held = pl.pallas_call(
        functools.partial(kernel, nrows, ncols, tile),
        out_shape=(jax.ShapeDtypeStruct(matrix.shape, F32), jax.ShapeDtypeStruct(panel.shape, F32)),
        in_specs=[hbm] * 3,
        out_specs=(vmem, vmem),
        scratch_shapes=[
            pltpu.VMEM((total, wide), F32),
            pltpu.VMEM((width, width), F32),
            pltpu.VMEM((nh, total, hw), F32),
            pltpu.VMEM((nh, wide, hw), F32),
            pltpu.VMEM((nh, total, hw), F32),
            pltpu.VMEM((nh, wide, hw), F32),
            pltpu.VMEM((nh, wide, hw), F32),
            pltpu.VMEM((nh, nrows, blk, hw), F32),
            pltpu.VMEM((width, hw), F32),
            pltpu.VMEM((nrows, width // 2, hw), F32),
            pltpu.VMEM((width // 2, hw), F32),
            pltpu.VMEM((width // 2, hw), F32),
            pltpu.VMEM((width, hw), F32),
            pltpu.VMEM((hw, hw), F32),
            pltpu.VMEM((nrows, hw // 2, hw), F32),
            pltpu.VMEM((hw // 2, hw), F32),
            pltpu.VMEM((hw, hw), F32),
            pltpu.VMEM((tiles, wide, tile), BF16),
            pltpu.VMEM((tiles, wide, tile), BF16),
            pltpu.VMEM((tiles, width, tile), BF16),
            pltpu.VMEM((tiles, width, tile), BF16),
            dma((nh + 2,)),
            dma((nh, lines)), dma((nh, lines)), dma((nh, lines)), dma((nh, lines)),
            dma((nh, nrows)), dma((nh, nrows)),
            dma((nh, lines)), dma((nh, nrows * group)),
            dma((nh, nrows * group)), dma((nh, nrows * group)),
            dma((nh, nrows)), dma((nh, nrows)),
            dma((nrows,)), dma((1,)), dma((nh, nrows)), dma((nh, nrows)), dma((nh,)), dma((nh,)),
        ],
        compiler_params=pltpu.CompilerParams(
            collective_id=0, has_side_effects=True, vmem_limit_bytes=limit),
    )(*(pltpu.with_memory_space_constraint(v, pltpu.HBM) for v in (matrix, panel, factor)))
    return pl.pallas_call(
        hand_out,
        out_shape=(jax.ShapeDtypeStruct(matrix.shape, F32), jax.ShapeDtypeStruct(panel.shape, F32)),
        in_specs=[vmem] * 2,
        out_specs=(vmem, vmem),
        compiler_params=pltpu.CompilerParams(vmem_limit_bytes=6 * total * wide * 4 + (1 << 20)),
    )(*held)


def solution(mesh):
    in_specs = (P("row", "col"), P(("row", "col"), None), P())
    out_specs = (P("row", "col"), P(("row", "col"), None))
    return jax.shard_map(
        functools.partial(per_device, mesh.shape["row"], mesh.shape["col"]),
        mesh=mesh, in_specs=in_specs, out_specs=out_specs, check_vma=False)
```

```python
import functools

import jax
import jax.numpy as jnp
from jax import lax
from jax.experimental import pallas as pl
from jax.experimental.pallas import tpu as pltpu
from jax.sharding import PartitionSpec as P

F32 = jnp.float32
BF16 = jnp.bfloat16
NN = (((1,), (0,)), ((), ()))
NT = (((1,), (1,)), ((), ()))


def split(x):
    high = x.astype(BF16)
    return high, (x - high.astype(F32)).astype(BF16)


def mult(a, b, dims=NN):
    dot = functools.partial(lax.dot_general, dimension_numbers=dims, preferred_element_type=F32)
    return dot(a[0], b[1]) + dot(a[1], b[0]) + dot(a[0], b[0])


def wide_of(ref, span):
    return jnp.concatenate([ref[0, span, :], ref[1, span, :]], axis=1)


def tile_loop(count, body):
    if count <= 2:
        for i in range(count):
            body(i)
    else:
        pl.loop(0, count)(body)


def kernel(nrows, ncols, tile, a_hbm, panel_hbm, t_hbm, out_ref, corr_ref,
           a_ref, t_ref, vr, vc, sr, sc, q, qin, kpart, kin, kpair, kside, kfull,
           lpart, lin, lpair, lfull,
           at_hi, at_lo, vt_hi, vt_lo,
           local_sem, v_send, v_recv, vf_send, vf_recv, q_send, q_recv,
           s_send, s_recv, sf_send, sf_recv, sc_send, sc_recv,
           vc_send, vc_recv, k_send, k_recv, kg_send, kg_recv):
    r, c = lax.axis_index("row"), lax.axis_index("col")
    lines = ncols // 2
    group = ncols // (2 * nrows)
    z, y = c // 2, c % 2
    total = a_ref.shape[0]
    nh, wide, hw = sc.shape
    blk, width = panel_hbm.shape
    tiles = total // tile
    mate = r + 1 - 2 * (r % 2)

    def rows(index, size):
        return pl.ds(pl.multiple_of(index * size, size), size)

    def peer(d):
        line = z
        for b in range(lines.bit_length()):
            if d >> b & 1:
                line = line + (1 << b) - (2 << b) * (z // (1 << b) % 2)
        return line

    def copy(src, dst, send, recv, row, col):
        return pltpu.make_async_remote_copy(
            src_ref=src, dst_ref=dst, send_sem=send, recv_sem=recv,
            device_id=(row, col), device_id_type=pl.DeviceIdType.MESH)

    sends = []

    def drain():
        for desc, when in sends:
            if when is None:
                desc.wait_send()
            else:
                pl.when(when)(desc.wait_send)
        sends.clear()

    def go(desc, when=None):
        if when is None:
            desc.start()
        else:
            pl.when(when)(desc.start)
        sends.append((desc, when))

    loads = [pltpu.make_async_copy(panel_hbm.at[:, pl.ds(h * hw, hw)], vr.at[h, rows(c, blk), :], local_sem.at[h])
             for h in range(nh)]
    loads.append(pltpu.make_async_copy(a_hbm, a_ref, local_sem.at[nh]))
    loads.append(pltpu.make_async_copy(t_hbm, t_ref, local_sem.at[nh + 1]))
    for load in loads:
        load.start()

    across = z * 2 + 1 - y
    target = z // group
    barrier = pltpu.get_barrier_semaphore()

    def greet(row, col):
        pl.semaphore_signal(barrier, inc=1, device_id=(row, col), device_id_type=pl.DeviceIdType.MESH)

    for d in range(1, lines):
        greet(r, peer(d) * 2 + y)
    greet(r, across)
    for d in range(1, nrows):
        greet(lax.rem(r + d, nrows), c)
    for d in range(1, nrows // 2):
        greet(lax.rem(r + 2 * d, nrows), across)
    for g in range(group):
        line = r * group + g

        @pl.when(z != line)
        def _():
            for d in range(1, nrows):
                greet(lax.rem(r + d, nrows), line * 2 + y)

    for h in range(nh):
        loads[h].wait()
    pl.semaphore_wait(barrier, lines + nrows + nrows // 2 - 2 + jnp.where(target == r, 0, lines - 1))

    order = list(range(1, lines))
    for h in range(nh):
        own = vr.at[h, rows(c, blk), :]
        go(copy(own, own, v_send.at[h, z], v_recv.at[h, z], r, across))
        for d in order:
            go(copy(own, own, v_send.at[h, peer(d)], v_recv.at[h, z], r, peer(d) * 2 + y))

    loads[nh].wait()

    def flip(i):
        high, low = split(a_ref[pl.ds(pl.multiple_of(i * tile, tile), tile), :].T)
        at_hi[i] = high
        at_lo[i] = low
    tile_loop(tiles, flip)
    loads[nh + 1].wait()
    t_two = split(t_ref[...])
    tt_two = split(t_ref[...].T)

    def arrived(h, line, side, recv):
        slot = vr.at[h, rows(line * 2 + side, blk), :]
        copy(slot, slot, v_send.at[h, line], recv.at[h, line], r, c).wait_recv()
        return slot

    for h in range(nh):
        for d in range(1, lines):
            line = peer(d)
            slot = arrived(h, line, y, v_recv)
            go(copy(slot, slot, vf_send.at[h, line], vf_recv.at[h, line], r, across))

    def reduce_product(h):
        for e in range(tiles):
            for d in (2 * e, 2 * e + 1):
                arrived(h, peer(d), 1 - y, vf_recv if d else v_recv)
            i = peer(2 * e) // 2
            part = mult((at_hi[i], at_lo[i]), split(vr[h, rows(i, tile), :]))
            q[h] = part if e == 0 else q[h] + part
        for d in range(1, nrows):
            other = lax.rem(r + d, nrows)
            go(copy(q.at[h, rows(other, blk), :], qin.at[h, d], q_send.at[h, d], q_recv.at[h, d], other, c))

    for h in range(nh):
        reduce_product(h)

    def turn(i):
        span = pl.ds(pl.multiple_of(i * tile, tile), tile)
        high, low = split(mult(tt_two, split(wide_of(vr, span)), NT))
        vt_hi[i] = high
        vt_lo[i] = low
    tile_loop(tiles, turn)

    place = lax.rem(c * nrows + r, ncols)
    here = r * group + lax.rem(z, group)
    products = []
    for h in range(nh):
        for d in range(1, nrows):
            copy(qin.at[h, d], qin.at[h, d], q_send.at[h, d], q_recv.at[h, d], r, c).wait_recv()
        product = q[h, rows(r, blk), :]
        for d in range(1, nrows):
            product = product + qin[h, d]
        products.append(split(product))
        scaled = None
        for g in range(h + 1):
            block = tuple(t[g * hw:(g + 1) * hw, h * hw:(h + 1) * hw] for t in t_two)
            term = mult(products[g], block)
            scaled = term if scaled is None else scaled + term
        mine = sc.at[h, rows(r, blk), :]
        mine[...] = scaled
        slot = sr.at[h, rows(place, blk), :]
        for d in order:
            go(copy(mine, slot, s_send.at[h, peer(d)], s_recv.at[h, here], target, peer(d) * 2 + y))
        for d in range(1, nrows // 2):
            go(copy(mine, mine, sc_send.at[h, 2 * d], sc_recv.at[h, 2 * d], lax.rem(r + 2 * d, nrows), c))
        go(copy(mine, mine, sc_send.at[h, 1], sc_recv.at[h, 1], mate, c))

    holder = c * nrows // ncols
    first_block = lax.rem(c * nrows, ncols)
    v_slice = vr.at[:, rows(first_block // nrows, wide), :]
    same = r % 2 == holder % 2
    def from_mate(h):
        for d in range(nrows // 2):
            slot = sc.at[h, rows(lax.rem(mate - 2 * d + nrows, nrows), blk), :]
            copy(slot, slot, sc_send.at[h, 2 * d + 1], sc_recv.at[h, 2 * d + 1], r, c).wait_recv()

    def forward_scaled(h):
        for d in range(1, nrows // 2):
            slot = sc.at[h, rows(lax.rem(r - 2 * d + nrows, nrows), blk), :]
            copy(slot, slot, sc_send.at[h, 2 * d], sc_recv.at[h, 2 * d], r, c).wait_recv()
            go(copy(slot, slot, sc_send.at[h, 2 * d + 1], sc_recv.at[h, 2 * d + 1], mate, c))
        pl.when(target == r)(functools.partial(from_mate, h))
        for g in range(group):
            line = r * group + g
            for d in range(nrows):
                j = lax.rem(r + d, nrows)
                at = j * group + g
                slot = sr.at[h, rows(lax.rem((line * 2 + y) * nrows + j, ncols), blk), :]
                held = sc.at[h, rows(j, blk), :]
                straight = copy(held, slot, sf_send.at[h, at], sf_recv.at[h, at], r, across)
                passed = copy(slot, slot, sf_send.at[h, at], sf_recv.at[h, at], r, across)
                came = copy(slot, slot, s_send.at[h, 0], s_recv.at[h, at], r, c)

                @pl.when(z == line)
                def _():
                    straight.start()
                    slot[...] = held[...]

                @pl.when(z != line)
                def _():
                    came.wait_recv()
                    passed.start()
                sends.append((passed, None))

    def gather_scaled(h):
        for g in range(group):
            line = r * group + g
            for j in range(nrows):
                at = j * group + g
                slot = sr.at[h, rows(lax.rem((line * 2 + 1 - y) * nrows + j, ncols), blk), :]
                copy(slot, slot, sf_send.at[h, at], sf_recv.at[h, at], r, c).wait_recv()

    def small(h, part, base):
        part[...] = jnp.zeros_like(part)
        for g in range(group):
            start = lax.rem(((r * group + g) * 2 + y) * nrows, ncols) * blk // tile
            for i in range(nrows * blk // tile):
                at = start + i
                part[...] += mult((vt_hi[at, base:, :], vt_lo[at, base:, :]), split(sr[h, rows(at, tile), :]))

    def pair_up(h, part, room, pair):
        size = pair.shape[0]
        go(copy(part.at[rows(mate % 2, size), :], room.at[0], k_send.at[h, 0], k_recv.at[h, 0], mate, c))
        copy(room.at[0], room.at[0], k_send.at[h, 0], k_recv.at[h, 0], r, c).wait_recv()
        pair[...] = part[rows(r % 2, size), :] + room[0]

    def spread(h, room, pair, slots):
        for i in slots:
            row, col = lax.rem(r + i // 2 * 2, nrows), across if i % 2 else c
            go(copy(pair, room.at[i], k_send.at[h, i], k_recv.at[h, i], row, col))

    def collect(h, room, pair, slots):
        for i in slots:
            copy(pair, room.at[i], k_send.at[h, i], k_recv.at[h, i], r, c).wait_recv()
        summed = pair[...]
        for i in slots:
            summed = summed + room[i]
        return summed

    def finish_half(h, full, summed):
        mine = full.at[rows(r % 2, summed.shape[0]), :]
        mine[...] = summed
        go(copy(mine, mine, kg_send.at[h], kg_recv.at[h], mate, c))

    def completed(h, pair, full):
        other = full.at[rows(mate % 2, pair.shape[0]), :]
        copy(other, other, kg_send.at[h], kg_recv.at[h], r, c).wait_recv()
        return split(full[...])

    older = sends[:]
    sends.clear()
    forward_scaled(0)
    small(0, kpart, 0)
    pair_up(0, kpart, kin, kpair)
    spread(0, kin, kpair, range(2, nrows, 2))
    forward_scaled(1)
    small(1, lpart, hw)
    pair_up(1, lpart, lin, lpair)
    spread(1, lin, lpair, range(1, nrows))
    for d in range(1, nrows // 2):
        go(copy(v_slice, vc, vc_send.at[d], vc_recv.at[0], lax.rem(r + 2 * d, nrows), c), r == holder)
    to_mate = copy(v_slice, vc, vc_send.at[0], vc_recv.at[0], mate, c)

    @pl.when(r == holder)
    def _():
        to_mate.start()
        vc[...] = v_slice[...]
    sends.append((to_mate, r == holder))


    newer = sends[:]
    sends[:] = older
    drain()
    sends[:] = newer
    gather_scaled(0)
    kside[...] = collect(0, kin, kpair, range(2, nrows, 2))
    spread(0, kin, kside, (1,))

    arrival = copy(vc, vc, vc_send.at[0], vc_recv.at[0], r, c)
    onward = copy(vc, vc, vc_send.at[0], vc_recv.at[0], mate, c)

    @pl.when(r != holder)
    def _():
        arrival.wait_recv()

        @pl.when(same)
        def _():
            onward.start()
    sends.append((onward, (r != holder) & same))
    gather_scaled(1)

    everything = pl.ds(0, wide)
    vc_two = split(wide_of(vc, everything))

    def first(i):
        span = pl.ds(pl.multiple_of(i * tile, tile), tile)
        out_ref[span, :] = a_ref[span, :] - mult(split(wide_of(sr, span)), vc_two, NT)
    tile_loop(tiles, first)

    finish_half(1, lfull, collect(1, lin, lpair, range(1, nrows)))
    finish_half(0, kfull, collect(0, kin, kside, (1,)))
    for h in range(nh):
        pl.when(target != r)(functools.partial(from_mate, h))
    completed(0, kpair, kfull)
    completed(1, lpair, lfull)
    left = kfull[...]
    right = jnp.concatenate([left[hw:, :].T, lfull[...]], axis=0)
    k_two = split(jnp.concatenate([left, right], axis=1))
    y_two = split(wide_of(sc, everything) - mult(vc_two, k_two))

    def second(i):
        span = pl.ds(pl.multiple_of(i * tile, tile), tile)
        out_ref[span, :] = out_ref[span, :] - mult(split(wide_of(vr, span)), y_two, NT)
    tile_loop(tiles, second)
    mine = rows(c, blk)
    corr_ref[...] = wide_of(sr, mine) - 0.5 * mult(split(wide_of(vr, mine)), k_two)
    drain()


def hand_out(held_ref, held_corr_ref, out_ref, corr_ref):
    out_ref[...] = held_ref[...]
    corr_ref[...] = held_corr_ref[...]


def per_device(nrows, ncols, matrix, panel, factor):
    total, wide = matrix.shape
    blk, width = panel.shape
    tile = 4 * blk
    tiles = total // tile
    group = ncols // (2 * nrows)
    lines = ncols // 2
    nh = 2
    hw = width // nh
    dma = pltpu.SemaphoreType.DMA
    vmem = pl.BlockSpec(memory_space=pltpu.VMEM)
    hbm = pl.BlockSpec(memory_space=pltpu.HBM)
    limit = 4 * (5 * total * wide + 4 * total * width + 4 * wide * width + 16 * width * width) + (8 << 20)
    held = pl.pallas_call(
        functools.partial(kernel, nrows, ncols, tile),
        out_shape=(jax.ShapeDtypeStruct(matrix.shape, F32), jax.ShapeDtypeStruct(panel.shape, F32)),
        in_specs=[hbm] * 3,
        out_specs=(vmem, vmem),
        scratch_shapes=[
            pltpu.VMEM((total, wide), F32),
            pltpu.VMEM((width, width), F32),
            pltpu.VMEM((nh, total, hw), F32),
            pltpu.VMEM((nh, wide, hw), F32),
            pltpu.VMEM((nh, total, hw), F32),
            pltpu.VMEM((nh, wide, hw), F32),
            pltpu.VMEM((nh, wide, hw), F32),
            pltpu.VMEM((nh, nrows, blk, hw), F32),
            pltpu.VMEM((width, hw), F32),
            pltpu.VMEM((nrows, width // 2, hw), F32),
            pltpu.VMEM((width // 2, hw), F32),
            pltpu.VMEM((width // 2, hw), F32),
            pltpu.VMEM((width, hw), F32),
            pltpu.VMEM((hw, hw), F32),
            pltpu.VMEM((nrows, hw // 2, hw), F32),
            pltpu.VMEM((hw // 2, hw), F32),
            pltpu.VMEM((hw, hw), F32),
            pltpu.VMEM((tiles, wide, tile), BF16),
            pltpu.VMEM((tiles, wide, tile), BF16),
            pltpu.VMEM((tiles, width, tile), BF16),
            pltpu.VMEM((tiles, width, tile), BF16),
            dma((nh + 2,)),
            dma((nh, lines)), dma((nh, lines)), dma((nh, lines)), dma((nh, lines)),
            dma((nh, nrows)), dma((nh, nrows)),
            dma((nh, lines)), dma((nh, nrows * group)),
            dma((nh, nrows * group)), dma((nh, nrows * group)),
            dma((nh, nrows)), dma((nh, nrows)),
            dma((nrows,)), dma((1,)), dma((nh, nrows)), dma((nh, nrows)), dma((nh,)), dma((nh,)),
        ],
        compiler_params=pltpu.CompilerParams(
            collective_id=0, has_side_effects=True, vmem_limit_bytes=limit),
    )(*(pltpu.with_memory_space_constraint(v, pltpu.HBM) for v in (matrix, panel, factor)))
    return pl.pallas_call(
        hand_out,
        out_shape=(jax.ShapeDtypeStruct(matrix.shape, F32), jax.ShapeDtypeStruct(panel.shape, F32)),
        in_specs=[vmem] * 2,
        out_specs=(vmem, vmem),
        compiler_params=pltpu.CompilerParams(vmem_limit_bytes=6 * total * wide * 4 + (1 << 20)),
    )(*held)


def solution(mesh):
    in_specs = (P("row", "col"), P(("row", "col"), None), P())
    out_specs = (P("row", "col"), P(("row", "col"), None))
    return jax.shard_map(
        functools.partial(per_device, mesh.shape["row"], mesh.shape["col"]),
        mesh=mesh, in_specs=in_specs, out_specs=out_specs, check_vma=False)
```

```python
import functools

import jax
import jax.numpy as jnp
from jax import lax
from jax.experimental import pallas as pl
from jax.experimental.pallas import tpu as pltpu
from jax.sharding import PartitionSpec as P

F32 = jnp.float32
BF16 = jnp.bfloat16
NN = (((1,), (0,)), ((), ()))
NT = (((1,), (1,)), ((), ()))


def split(x):
    high = x.astype(BF16)
    return high, (x - high.astype(F32)).astype(BF16)


def mult(a, b, dims=NN):
    dot = functools.partial(lax.dot_general, dimension_numbers=dims, preferred_element_type=F32)
    return dot(a[0], b[1]) + dot(a[1], b[0]) + dot(a[0], b[0])


def wide_of(ref, span):
    return jnp.concatenate([ref[0, span, :], ref[1, span, :]], axis=1)


def tile_loop(count, body):
    if count <= 2:
        for i in range(count):
            body(i)
    else:
        pl.loop(0, count)(body)


def kernel(nrows, ncols, tile, a_hbm, panel_hbm, t_hbm, out_ref, corr_ref, v_hi, v_lo, y_hi, y_lo,
           a_ref, t_ref, vr, vc, sr, sc, q, qin, kpart, kin, kpair, kside, kfull,
           lpart, lin, lpair, lfull,
           at_hi, at_lo, vt_hi, vt_lo,
           local_sem, v_send, v_recv, vf_send, vf_recv, q_send, q_recv,
           s_send, s_recv, sf_send, sf_recv, sc_send, sc_recv,
           vc_send, vc_recv, k_send, k_recv, kg_send, kg_recv):
    r, c = lax.axis_index("row"), lax.axis_index("col")
    lines = ncols // 2
    group = ncols // (2 * nrows)
    z, y = c // 2, c % 2
    total = a_ref.shape[0]
    nh, wide, hw = sc.shape
    blk, width = panel_hbm.shape
    tiles = total // tile
    mate = r + 1 - 2 * (r % 2)

    def rows(index, size):
        return pl.ds(pl.multiple_of(index * size, size), size)

    def peer(d):
        line = z
        for b in range(lines.bit_length()):
            if d >> b & 1:
                line = line + (1 << b) - (2 << b) * (z // (1 << b) % 2)
        return line

    def copy(src, dst, send, recv, row, col):
        return pltpu.make_async_remote_copy(
            src_ref=src, dst_ref=dst, send_sem=send, recv_sem=recv,
            device_id=(row, col), device_id_type=pl.DeviceIdType.MESH)

    sends = []

    def drain():
        for desc, when in sends:
            if when is None:
                desc.wait_send()
            else:
                pl.when(when)(desc.wait_send)
        sends.clear()

    def go(desc, when=None):
        if when is None:
            desc.start()
        else:
            pl.when(when)(desc.start)
        sends.append((desc, when))

    loads = [pltpu.make_async_copy(panel_hbm.at[:, pl.ds(h * hw, hw)], vr.at[h, rows(c, blk), :], local_sem.at[h])
             for h in range(nh)]
    loads.append(pltpu.make_async_copy(a_hbm, a_ref, local_sem.at[nh]))
    loads.append(pltpu.make_async_copy(t_hbm, t_ref, local_sem.at[nh + 1]))
    for load in loads:
        load.start()

    across = z * 2 + 1 - y
    target = z // group
    barrier = pltpu.get_barrier_semaphore()

    def greet(row, col):
        pl.semaphore_signal(barrier, inc=1, device_id=(row, col), device_id_type=pl.DeviceIdType.MESH)

    for d in range(1, lines):
        greet(r, peer(d) * 2 + y)
    greet(r, across)
    for d in range(1, nrows):
        greet(lax.rem(r + d, nrows), c)
    for h in range(nh):
        loads[h].wait()
    pl.semaphore_wait(barrier, lines + nrows - 1)

    order = list(range(1, lines))
    for h in range(nh):
        own = vr.at[h, rows(c, blk), :]
        go(copy(own, own, v_send.at[h, z], v_recv.at[h, z], r, across))
        for d in order:
            go(copy(own, own, v_send.at[h, peer(d)], v_recv.at[h, z], r, peer(d) * 2 + y))

    loads[nh].wait()

    def flip(i):
        high, low = split(a_ref[pl.ds(pl.multiple_of(i * tile, tile), tile), :].T)
        at_hi[i] = high
        at_lo[i] = low
    tile_loop(tiles, flip)
    loads[nh + 1].wait()
    t_two = split(t_ref[...])
    tt_two = split(t_ref[...].T)

    def arrived(h, line, side, recv):
        slot = vr.at[h, rows(line * 2 + side, blk), :]
        copy(slot, slot, v_send.at[h, line], recv.at[h, line], r, c).wait_recv()
        return slot

    for h in range(nh):
        for d in range(1, lines):
            line = peer(d)
            slot = arrived(h, line, y, v_recv)
            go(copy(slot, slot, vf_send.at[h, line], vf_recv.at[h, line], r, across))

    holder = c * nrows // ncols
    first_block = lax.rem(c * nrows, ncols)
    same = r % 2 == holder % 2

    def hand_panel(h):
        held = vr.at[h, rows(first_block // nrows, wide), :]
        kept = vc.at[h]
        for d in range(1, nrows // 2):
            go(copy(held, kept, vc_send.at[h, d], vc_recv.at[h], lax.rem(r + 2 * d, nrows), c), r == holder)
        go(copy(held, kept, vc_send.at[h, 0], vc_recv.at[h], mate, c), r == holder)

        @pl.when(r == holder)
        def _():
            kept[...] = held[...]

    def pass_panel(h):
        kept = vc.at[h]

        @pl.when(r != holder)
        def _():
            copy(kept, kept, vc_send.at[h, 0], vc_recv.at[h], r, c).wait_recv()
        go(copy(kept, kept, vc_send.at[h, 0], vc_recv.at[h], mate, c), (r != holder) & same)

    def reduce_product(h):
        for e in range(tiles):
            for d in (2 * e, 2 * e + 1):
                arrived(h, peer(d), 1 - y, vf_recv if d else v_recv)
            i = peer(2 * e) // 2
            part = mult((at_hi[i], at_lo[i]), split(vr[h, rows(i, tile), :]))
            q[h] = part if e == 0 else q[h] + part
        for d in range(1, nrows):
            other = lax.rem(r + d, nrows)
            go(copy(q.at[h, rows(other, blk), :], qin.at[h, d], q_send.at[h, d], q_recv.at[h, d], other, c))

    reduce_product(0)
    hand_panel(0)
    reduce_product(1)

    def turn(i):
        span = pl.ds(pl.multiple_of(i * tile, tile), tile)
        v_two = split(wide_of(vr, span))
        v_hi[span, :], v_lo[span, :] = v_two
        high, low = split(mult(tt_two, v_two, NT))
        vt_hi[i] = high
        vt_lo[i] = low
    tile_loop(tiles, turn)

    place = lax.rem(c * nrows + r, ncols)
    here = r * group + lax.rem(z, group)
    products = []
    for h in range(nh):
        for d in range(1, nrows):
            copy(qin.at[h, d], qin.at[h, d], q_send.at[h, d], q_recv.at[h, d], r, c).wait_recv()
        product = q[h, rows(r, blk), :]
        for d in range(1, nrows):
            product = product + qin[h, d]
        products.append(split(product))
        scaled = None
        for g in range(h + 1):
            block = tuple(t[g * hw:(g + 1) * hw, h * hw:(h + 1) * hw] for t in t_two)
            term = mult(products[g], block)
            scaled = term if scaled is None else scaled + term
        mine = sc.at[h, rows(r, blk), :]
        mine[...] = scaled
        slot = sr.at[h, rows(place, blk), :]
        for d in order:
            go(copy(mine, slot, s_send.at[h, peer(d)], s_recv.at[h, here], target, peer(d) * 2 + y))
        for d in range(1, nrows // 2):
            go(copy(mine, mine, sc_send.at[h, 2 * d], sc_recv.at[h, 2 * d], lax.rem(r + 2 * d, nrows), c))
        go(copy(mine, mine, sc_send.at[h, 1], sc_recv.at[h, 1], mate, c))

    def from_mate(h):
        for d in range(nrows // 2):
            slot = sc.at[h, rows(lax.rem(mate - 2 * d + nrows, nrows), blk), :]
            copy(slot, slot, sc_send.at[h, 2 * d + 1], sc_recv.at[h, 2 * d + 1], r, c).wait_recv()

    def forward_scaled(h):
        for d in range(1, nrows // 2):
            slot = sc.at[h, rows(lax.rem(r - 2 * d + nrows, nrows), blk), :]
            copy(slot, slot, sc_send.at[h, 2 * d], sc_recv.at[h, 2 * d], r, c).wait_recv()
            go(copy(slot, slot, sc_send.at[h, 2 * d + 1], sc_recv.at[h, 2 * d + 1], mate, c))
        pl.when(target == r)(functools.partial(from_mate, h))
        for g in range(group):
            line = r * group + g
            for d in range(nrows):
                j = lax.rem(r + d, nrows)
                at = j * group + g
                slot = sr.at[h, rows(lax.rem((line * 2 + y) * nrows + j, ncols), blk), :]
                held = sc.at[h, rows(j, blk), :]
                straight = copy(held, slot, sf_send.at[h, at], sf_recv.at[h, at], r, across)
                passed = copy(slot, slot, sf_send.at[h, at], sf_recv.at[h, at], r, across)
                came = copy(slot, slot, s_send.at[h, 0], s_recv.at[h, at], r, c)

                @pl.when(z == line)
                def _():
                    straight.start()
                    slot[...] = held[...]

                @pl.when(z != line)
                def _():
                    came.wait_recv()
                    passed.start()
                sends.append((passed, None))

    def gather_scaled(h):
        for g in range(group):
            line = r * group + g
            for j in range(nrows):
                at = j * group + g
                slot = sr.at[h, rows(lax.rem((line * 2 + 1 - y) * nrows + j, ncols), blk), :]
                copy(slot, slot, sf_send.at[h, at], sf_recv.at[h, at], r, c).wait_recv()

    def small(h, part, base):
        part[...] = jnp.zeros_like(part)
        for g in range(group):
            start = lax.rem(((r * group + g) * 2 + y) * nrows, ncols) * blk // tile
            for i in range(nrows * blk // tile):
                at = start + i
                part[...] += mult((vt_hi[at, base:, :], vt_lo[at, base:, :]), split(sr[h, rows(at, tile), :]))

    def pair_up(h, part, room, pair):
        size = pair.shape[0]
        go(copy(part.at[rows(mate % 2, size), :], room.at[0], k_send.at[h, 0], k_recv.at[h, 0], mate, c))
        copy(room.at[0], room.at[0], k_send.at[h, 0], k_recv.at[h, 0], r, c).wait_recv()
        pair[...] = part[rows(r % 2, size), :] + room[0]

    def spread(h, room, pair, slots):
        for i in slots:
            row, col = lax.rem(r + i // 2 * 2, nrows), across if i % 2 else c
            go(copy(pair, room.at[i], k_send.at[h, i], k_recv.at[h, i], row, col))

    def collect(h, room, pair, slots):
        for i in slots:
            copy(pair, room.at[i], k_send.at[h, i], k_recv.at[h, i], r, c).wait_recv()
        summed = pair[...]
        for i in slots:
            summed = summed + room[i]
        return summed

    def finish_half(h, full, summed):
        mine = full.at[rows(r % 2, summed.shape[0]), :]
        mine[...] = summed
        go(copy(mine, mine, kg_send.at[h], kg_recv.at[h], mate, c))

    def completed(h, pair, full):
        other = full.at[rows(mate % 2, pair.shape[0]), :]
        copy(other, other, kg_send.at[h], kg_recv.at[h], r, c).wait_recv()
        return split(full[...])

    hand_panel(1)
    older = sends[:]
    sends.clear()
    forward_scaled(0)
    small(0, kpart, 0)
    pair_up(0, kpart, kin, kpair)
    spread(0, kin, kpair, range(2, nrows, 2))
    forward_scaled(1)
    small(1, lpart, hw)
    pair_up(1, lpart, lin, lpair)
    spread(1, lin, lpair, range(1, nrows))
    pass_panel(0)


    newer = sends[:]
    sends[:] = older
    drain()
    sends[:] = newer
    kside[...] = collect(0, kin, kpair, range(2, nrows, 2))
    spread(0, kin, kside, (1,))
    gather_scaled(0)

    pass_panel(1)
    gather_scaled(1)

    everything = pl.ds(0, wide)
    vc_two = split(wide_of(vc, everything))

    def first(i):
        span = pl.ds(pl.multiple_of(i * tile, tile), tile)
        out_ref[span, :] = a_ref[span, :] - mult(split(wide_of(sr, span)), vc_two, NT)
    tile_loop(tiles, first)

    finish_half(1, lfull, collect(1, lin, lpair, range(1, nrows)))
    finish_half(0, kfull, collect(0, kin, kside, (1,)))
    for h in range(nh):
        pl.when(target != r)(functools.partial(from_mate, h))
    completed(0, kpair, kfull)
    completed(1, lpair, lfull)
    left = kfull[...]
    right = jnp.concatenate([left[hw:, :].T, lfull[...]], axis=0)
    k_two = split(jnp.concatenate([left, right], axis=1))
    y_hi[...], y_lo[...] = split(wide_of(sc, everything) - mult(vc_two, k_two))
    mine = rows(c, blk)
    corr_ref[...] = wide_of(sr, mine) - 0.5 * mult((v_hi[mine, :], v_lo[mine, :]), k_two)
    drain()


def hand_out(tile, held_ref, held_corr_ref, v_hi, v_lo, y_hi, y_lo, out_hbm, corr_hbm, stage, sem):
    tiles = held_ref.shape[0] // tile
    copies = [pltpu.make_async_copy(held_corr_ref, corr_hbm, sem.at[tiles])]
    copies[0].start()
    for i in range(tiles):
        span = pl.ds(i * tile, tile)
        stage[span, :] = held_ref[span, :] - mult((v_hi[span, :], v_lo[span, :]), (y_hi[...], y_lo[...]), NT)
        copies.append(pltpu.make_async_copy(stage.at[span, :], out_hbm.at[span, :], sem.at[i]))
        copies[-1].start()
    for copy in copies:
        copy.wait()


def per_device(nrows, ncols, matrix, panel, factor):
    total, wide = matrix.shape
    blk, width = panel.shape
    tile = 4 * blk
    tiles = total // tile
    group = ncols // (2 * nrows)
    lines = ncols // 2
    nh = 2
    hw = width // nh
    dma = pltpu.SemaphoreType.DMA
    vmem = pl.BlockSpec(memory_space=pltpu.VMEM)
    hbm = pl.BlockSpec(memory_space=pltpu.HBM)
    limit = 4 * (5 * total * wide + 4 * total * width + 4 * wide * width + 16 * width * width) + (8 << 20)
    held = pl.pallas_call(
        functools.partial(kernel, nrows, ncols, tile),
        out_shape=(jax.ShapeDtypeStruct(matrix.shape, F32), jax.ShapeDtypeStruct(panel.shape, F32),
                   jax.ShapeDtypeStruct((total, width), BF16), jax.ShapeDtypeStruct((total, width), BF16),
                   jax.ShapeDtypeStruct((wide, width), BF16), jax.ShapeDtypeStruct((wide, width), BF16)),
        in_specs=[hbm] * 3,
        out_specs=(vmem,) * 6,
        scratch_shapes=[
            pltpu.VMEM((total, wide), F32),
            pltpu.VMEM((width, width), F32),
            pltpu.VMEM((nh, total, hw), F32),
            pltpu.VMEM((nh, wide, hw), F32),
            pltpu.VMEM((nh, total, hw), F32),
            pltpu.VMEM((nh, wide, hw), F32),
            pltpu.VMEM((nh, wide, hw), F32),
            pltpu.VMEM((nh, nrows, blk, hw), F32),
            pltpu.VMEM((width, hw), F32),
            pltpu.VMEM((nrows, width // 2, hw), F32),
            pltpu.VMEM((width // 2, hw), F32),
            pltpu.VMEM((width // 2, hw), F32),
            pltpu.VMEM((width, hw), F32),
            pltpu.VMEM((hw, hw), F32),
            pltpu.VMEM((nrows, hw // 2, hw), F32),
            pltpu.VMEM((hw // 2, hw), F32),
            pltpu.VMEM((hw, hw), F32),
            pltpu.VMEM((tiles, wide, tile), BF16),
            pltpu.VMEM((tiles, wide, tile), BF16),
            pltpu.VMEM((tiles, width, tile), BF16),
            pltpu.VMEM((tiles, width, tile), BF16),
            dma((nh + 2,)),
            dma((nh, lines)), dma((nh, lines)), dma((nh, lines)), dma((nh, lines)),
            dma((nh, nrows)), dma((nh, nrows)),
            dma((nh, lines)), dma((nh, nrows * group)),
            dma((nh, nrows * group)), dma((nh, nrows * group)),
            dma((nh, nrows)), dma((nh, nrows)),
            dma((nh, nrows)), dma((nh,)), dma((nh, nrows)), dma((nh, nrows)), dma((nh,)), dma((nh,)),
        ],
        compiler_params=pltpu.CompilerParams(
            collective_id=0, has_side_effects=True, vmem_limit_bytes=limit),
    )(*(pltpu.with_memory_space_constraint(v, pltpu.HBM) for v in (matrix, panel, factor)))
    return pl.pallas_call(
        functools.partial(hand_out, tile),
        out_shape=(jax.ShapeDtypeStruct(matrix.shape, F32), jax.ShapeDtypeStruct(panel.shape, F32)),
        in_specs=[vmem] * 6,
        out_specs=(hbm, hbm),
        scratch_shapes=[pltpu.VMEM((total, wide), F32), dma((tiles + 1,))],
        compiler_params=pltpu.CompilerParams(vmem_limit_bytes=8 * total * wide * 4 + (4 << 20)),
    )(*held)


def solution(mesh):
    in_specs = (P("row", "col"), P(("row", "col"), None), P())
    out_specs = (P("row", "col"), P(("row", "col"), None))
    return jax.shard_map(
        functools.partial(per_device, mesh.shape["row"], mesh.shape["col"]),
        mesh=mesh, in_specs=in_specs, out_specs=out_specs, check_vma=False)
```

```python
import functools

import jax
import jax.numpy as jnp
from jax import lax
from jax.experimental import pallas as pl
from jax.experimental.pallas import tpu as pltpu
from jax.sharding import PartitionSpec as P

F32 = jnp.float32
BF16 = jnp.bfloat16
NN = (((1,), (0,)), ((), ()))
NT = (((1,), (1,)), ((), ()))


def split(x):
    high = x.astype(BF16)
    return high, (x - high.astype(F32)).astype(BF16)


def mult(a, b, dims=NN):
    dot = functools.partial(lax.dot_general, dimension_numbers=dims, preferred_element_type=F32)
    return dot(a[0], b[1]) + dot(a[1], b[0]) + dot(a[0], b[0])


def wide_of(ref, span):
    return jnp.concatenate([ref[0, span, :], ref[1, span, :]], axis=1)


def tile_loop(count, body):
    if count <= 2:
        for i in range(count):
            body(i)
    else:
        pl.loop(0, count)(body)


def kernel(nrows, ncols, tile, a_hbm, panel_hbm, t_hbm, out_ref, corr_ref, v_hi, v_lo, y_hi, y_lo,
           a_ref, t_ref, vr, vc, sr, sc, q, qin, kpart, kin, kpair, kside, kfull,
           lpart, lin, lpair, lfull,
           at_hi, at_lo, vt_hi, vt_lo,
           local_sem, v_send, v_recv, vf_send, vf_recv, q_send, q_recv,
           s_send, s_recv, sf_send, sf_recv, sc_send, sc_recv,
           vc_send, vc_recv, k_send, k_recv, kg_send, kg_recv):
    r, c = lax.axis_index("row"), lax.axis_index("col")
    lines = ncols // 2
    group = ncols // (2 * nrows)
    z, y = c // 2, c % 2
    total = a_ref.shape[0]
    nh, wide, hw = sc.shape
    blk, width = panel_hbm.shape
    tiles = total // tile
    mate = r + 1 - 2 * (r % 2)

    def rows(index, size):
        return pl.ds(pl.multiple_of(index * size, size), size)

    def peer(d):
        line = z
        for b in range(lines.bit_length()):
            if d >> b & 1:
                line = line + (1 << b) - (2 << b) * (z // (1 << b) % 2)
        return line

    def copy(src, dst, send, recv, row, col):
        return pltpu.make_async_remote_copy(
            src_ref=src, dst_ref=dst, send_sem=send, recv_sem=recv,
            device_id=(row, col), device_id_type=pl.DeviceIdType.MESH)

    def go(desc, when=None):
        if when is None:
            desc.start()
        else:
            pl.when(when)(desc.start)

    def sent(ref, sem):
        copy(ref, ref, sem, kg_recv.at[0], r, c).wait_send()

    def landed(ref, sem):
        copy(ref, ref, kg_send.at[0], sem, r, c).wait_recv()

    def some(ref, h, count):
        return ref.at[h, pl.ds(0, count * blk), :]

    loads = [pltpu.make_async_copy(panel_hbm.at[:, pl.ds(h * hw, hw)], vr.at[h, rows(c, blk), :], local_sem.at[h])
             for h in range(nh)]
    loads.append(pltpu.make_async_copy(a_hbm, a_ref, local_sem.at[nh]))
    loads.append(pltpu.make_async_copy(t_hbm, t_ref, local_sem.at[nh + 1]))
    for load in loads[:nh]:
        load.start()

    across = z * 2 + 1 - y
    target = z // group
    barrier = pltpu.get_barrier_semaphore()

    def greet(row, col):
        pl.semaphore_signal(barrier, inc=1, device_id=(row, col), device_id_type=pl.DeviceIdType.MESH)

    for d in reversed(range(1, lines)):
        greet(r, peer(d) * 2 + y)
    greet(r, across)
    for d in range(1, nrows):
        greet(lax.rem(r + d, nrows), c)
    for load in loads[nh:]:
        load.start()
    for h in range(nh):
        loads[h].wait()
    pl.semaphore_wait(barrier, lines + nrows - 1)

    order = list(range(1, lines))
    for h in range(nh):
        own = vr.at[h, rows(c, blk), :]
        go(copy(own, own, v_send.at[h], v_recv.at[h, z], r, across))
        for d in order:
            go(copy(own, own, v_send.at[h], v_recv.at[h, z], r, peer(d) * 2 + y))

    loads[nh].wait()

    def flip(i):
        high, low = split(a_ref[pl.ds(pl.multiple_of(i * tile, tile), tile), :].T)
        at_hi[i] = high
        at_lo[i] = low
    tile_loop(tiles, flip)
    loads[nh + 1].wait()
    t_two = split(t_ref[...])
    tt_two = split(t_ref[...].T)

    for h in range(nh):
        for d in range(1, lines):
            line = peer(d)
            slot = vr.at[h, rows(line * 2 + y, blk), :]
            landed(slot, v_recv.at[h, line])
            go(copy(slot, slot, vf_send.at[h], vf_recv.at[h, d // 2], r, across))

    holder = c * nrows // ncols
    first_block = lax.rem(c * nrows, ncols)
    same = r % 2 == holder % 2

    def hand_panel(h):
        held = vr.at[h, rows(first_block // nrows, wide), :]
        kept = vc.at[h]
        for d in range(1, nrows // 2):
            go(copy(held, kept, vc_send.at[h], vc_recv.at[h], lax.rem(r + 2 * d, nrows), c), r == holder)
        go(copy(held, kept, vc_send.at[h], vc_recv.at[h], mate, c), r == holder)

        @pl.when(r == holder)
        def _():
            kept[...] = held[...]

    def pass_panel(h):
        kept = vc.at[h]

        @pl.when(r != holder)
        def _():
            landed(kept, vc_recv.at[h])
        go(copy(kept, kept, vc_send.at[h], vc_recv.at[h], mate, c), (r != holder) & same)

    def reduce_product(h):
        for e in range(tiles):
            if e == 0:
                landed(some(vr, h, 1), v_recv.at[h, z])
            landed(some(vr, h, 2 if e else 1), vf_recv.at[h, e])
            i = peer(2 * e) // 2
            part = mult((at_hi[i], at_lo[i]), split(vr[h, rows(i, tile), :]))
            q[h] = part if e == 0 else q[h] + part
        for d in range(1, nrows):
            other = lax.rem(r + d, nrows)
            go(copy(q.at[h, rows(other, blk), :], qin.at[h, d], q_send.at[h], q_recv.at[h], other, c))

    reduce_product(0)
    hand_panel(0)
    reduce_product(1)

    def turn(i):
        span = pl.ds(pl.multiple_of(i * tile, tile), tile)
        v_two = split(wide_of(vr, span))
        v_hi[span, :], v_lo[span, :] = v_two
        high, low = split(mult(tt_two, v_two, NT))
        vt_hi[i] = high
        vt_lo[i] = low
    tile_loop(tiles, turn)

    place = lax.rem(c * nrows + r, ncols)
    here = r * group + lax.rem(z, group)
    products = []
    for h in range(nh):
        landed(qin.at[h, pl.ds(1, nrows - 1)], q_recv.at[h])
        product = q[h, rows(r, blk), :]
        for d in range(1, nrows):
            product = product + qin[h, d]
        products.append(split(product))
        scaled = None
        for g in range(h + 1):
            block = tuple(t[g * hw:(g + 1) * hw, h * hw:(h + 1) * hw] for t in t_two)
            term = mult(products[g], block)
            scaled = term if scaled is None else scaled + term
        mine = sc.at[h, rows(r, blk), :]
        mine[...] = scaled
        slot = sr.at[h, rows(place, blk), :]
        for d in order:
            go(copy(mine, slot, s_send.at[h], s_recv.at[h, here], target, peer(d) * 2 + y))
        for d in range(1, nrows // 2):
            go(copy(mine, mine, sc_send.at[h], sc_recv.at[h, d], lax.rem(r + 2 * d, nrows), c))
        go(copy(mine, mine, sc_send.at[h], sc_recv.at[h, 0], mate, c))

    def from_mate(h):
        landed(some(sc, h, nrows // 2), sc_recv.at[h, 0])

    def forward_scaled(h):
        for d in range(1, nrows // 2):
            slot = sc.at[h, rows(lax.rem(r - 2 * d + nrows, nrows), blk), :]
            landed(slot, sc_recv.at[h, d])
            go(copy(slot, slot, sc_send.at[h], sc_recv.at[h, 0], mate, c))
        pl.when(target == r)(functools.partial(from_mate, h))
        for g in range(group):
            line = r * group + g
            for d in range(nrows):
                j = lax.rem(r + d, nrows)
                at = j * group + g
                slot = sr.at[h, rows(lax.rem((line * 2 + y) * nrows + j, ncols), blk), :]
                held = sc.at[h, rows(j, blk), :]
                straight = copy(held, slot, sf_send.at[h], sf_recv.at[h], r, across)
                passed = copy(slot, slot, sf_send.at[h], sf_recv.at[h], r, across)

                @pl.when(z == line)
                def _():
                    straight.start()
                    slot[...] = held[...]

                @pl.when(z != line)
                def _():
                    landed(slot, s_recv.at[h, at])
                    passed.start()

    def gather_scaled(h):
        landed(some(sr, h, nrows * group), sf_recv.at[h])

    def small(h, part, base):
        part[...] = jnp.zeros_like(part)
        for g in range(group):
            start = lax.rem(((r * group + g) * 2 + y) * nrows, ncols) * blk // tile
            for i in range(nrows * blk // tile):
                at = start + i
                part[...] += mult((vt_hi[at, base:, :], vt_lo[at, base:, :]), split(sr[h, rows(at, tile), :]))

    def pair_up(h, part, room, pair):
        size = pair.shape[0]
        go(copy(part.at[rows(mate % 2, size), :], room.at[0], k_send.at[h], k_recv.at[h, 0], mate, c))
        landed(room.at[0], k_recv.at[h, 0])
        pair[...] = part[rows(r % 2, size), :] + room[0]

    def spread(h, step, room, pair, slots):
        for i in slots:
            row, col = lax.rem(r + i // 2 * 2, nrows), across if i % 2 else c
            go(copy(pair, room.at[i], k_send.at[h], k_recv.at[h, step], row, col))

    def collect(h, step, room, pair, slots):
        landed(room.at[pl.ds(0, len(slots))], k_recv.at[h, step])
        summed = pair[...]
        for i in slots:
            summed = summed + room[i]
        return summed

    def finish_half(h, full, summed):
        mine = full.at[rows(r % 2, summed.shape[0]), :]
        mine[...] = summed
        go(copy(mine, mine, kg_send.at[h], kg_recv.at[h], mate, c))

    def completed(h, pair, full):
        other = full.at[rows(mate % 2, pair.shape[0]), :]
        landed(other, kg_recv.at[h])
        return split(full[...])

    hand_panel(1)
    forward_scaled(0)
    small(0, kpart, 0)
    pair_up(0, kpart, kin, kpair)
    spread(0, 1, kin, kpair, range(2, nrows, 2))
    forward_scaled(1)
    small(1, lpart, hw)
    pair_up(1, lpart, lin, lpair)
    spread(1, 1, lin, lpair, range(1, nrows))
    pass_panel(0)
    for h in range(nh):
        sent(some(vr, h, lines), v_send.at[h])
        sent(some(vr, h, lines - 1), vf_send.at[h])
        sent(some(q, h, nrows - 1), q_send.at[h])
        sent(some(sr, h, lines - 1), s_send.at[h])
        sent(some(sc, h, nrows - 1), sc_send.at[h])
    kside[...] = collect(0, 1, kin, kpair, range(2, nrows, 2))
    spread(0, 2, kin, kside, (1,))
    gather_scaled(0)

    pass_panel(1)
    gather_scaled(1)

    everything = pl.ds(0, wide)
    vc_two = split(wide_of(vc, everything))

    def first(i):
        span = pl.ds(pl.multiple_of(i * tile, tile), tile)
        out_ref[span, :] = a_ref[span, :] - mult(split(wide_of(sr, span)), vc_two, NT)
    tile_loop(tiles, first)

    finish_half(1, lfull, collect(1, 1, lin, lpair, range(1, nrows)))
    finish_half(0, kfull, collect(0, 2, kin, kside, (1,)))
    for h in range(nh):
        pl.when(target != r)(functools.partial(from_mate, h))
    completed(0, kpair, kfull)
    completed(1, lpair, lfull)
    left = kfull[...]
    right = jnp.concatenate([left[hw:, :].T, lfull[...]], axis=0)
    k_two = split(jnp.concatenate([left, right], axis=1))
    y_hi[...], y_lo[...] = split(wide_of(sc, everything) - mult(vc_two, k_two))
    mine = rows(c, blk)
    corr_ref[...] = wide_of(sr, mine) - 0.5 * mult((v_hi[mine, :], v_lo[mine, :]), k_two)
    for h, room, count in ((0, kin, nrows // 2 + 1), (1, lin, nrows)):
        sent(some(sr, h, nrows * group), sf_send.at[h])
        sent(room.at[pl.ds(0, count)], k_send.at[h])

        @pl.when(r == holder)
        def _():
            sent(vr.at[h, pl.ds(0, nrows // 2 * wide), :], vc_send.at[h])

        @pl.when((r != holder) & same)
        def _():
            sent(vc.at[h], vc_send.at[h])
    sent(kfull.at[pl.ds(0, kpair.shape[0]), :], kg_send.at[0])
    sent(lfull.at[pl.ds(0, lpair.shape[0]), :], kg_send.at[1])


def hand_out(tile, held_ref, held_corr_ref, v_hi, v_lo, y_hi, y_lo, out_hbm, corr_hbm, stage, sem):
    tiles = held_ref.shape[0] // tile
    copies = [pltpu.make_async_copy(held_corr_ref, corr_hbm, sem.at[tiles])]
    copies[0].start()
    for i in range(tiles):
        span = pl.ds(i * tile, tile)
        stage[span, :] = held_ref[span, :] - mult((v_hi[span, :], v_lo[span, :]), (y_hi[...], y_lo[...]), NT)
        copies.append(pltpu.make_async_copy(stage.at[span, :], out_hbm.at[span, :], sem.at[i]))
        copies[-1].start()
    for copy in copies:
        copy.wait()


def per_device(nrows, ncols, matrix, panel, factor):
    total, wide = matrix.shape
    blk, width = panel.shape
    tile = 4 * blk
    tiles = total // tile
    group = ncols // (2 * nrows)
    lines = ncols // 2
    nh = 2
    hw = width // nh
    dma = pltpu.SemaphoreType.DMA
    vmem = pl.BlockSpec(memory_space=pltpu.VMEM)
    hbm = pl.BlockSpec(memory_space=pltpu.HBM)
    limit = 4 * (5 * total * wide + 4 * total * width + 4 * wide * width + 16 * width * width) + (8 << 20)
    held = pl.pallas_call(
        functools.partial(kernel, nrows, ncols, tile),
        out_shape=(jax.ShapeDtypeStruct(matrix.shape, F32), jax.ShapeDtypeStruct(panel.shape, F32),
                   jax.ShapeDtypeStruct((total, width), BF16), jax.ShapeDtypeStruct((total, width), BF16),
                   jax.ShapeDtypeStruct((wide, width), BF16), jax.ShapeDtypeStruct((wide, width), BF16)),
        in_specs=[hbm] * 3,
        out_specs=(vmem,) * 6,
        scratch_shapes=[
            pltpu.VMEM((total, wide), F32),
            pltpu.VMEM((width, width), F32),
            pltpu.VMEM((nh, total, hw), F32),
            pltpu.VMEM((nh, wide, hw), F32),
            pltpu.VMEM((nh, total, hw), F32),
            pltpu.VMEM((nh, wide, hw), F32),
            pltpu.VMEM((nh, wide, hw), F32),
            pltpu.VMEM((nh, nrows, blk, hw), F32),
            pltpu.VMEM((width, hw), F32),
            pltpu.VMEM((nrows, width // 2, hw), F32),
            pltpu.VMEM((width // 2, hw), F32),
            pltpu.VMEM((width // 2, hw), F32),
            pltpu.VMEM((width, hw), F32),
            pltpu.VMEM((hw, hw), F32),
            pltpu.VMEM((nrows, hw // 2, hw), F32),
            pltpu.VMEM((hw // 2, hw), F32),
            pltpu.VMEM((hw, hw), F32),
            pltpu.VMEM((tiles, wide, tile), BF16),
            pltpu.VMEM((tiles, wide, tile), BF16),
            pltpu.VMEM((tiles, width, tile), BF16),
            pltpu.VMEM((tiles, width, tile), BF16),
            dma((nh + 2,)),
            dma((nh,)), dma((nh, lines)), dma((nh,)), dma((nh, lines // 2)),
            dma((nh,)), dma((nh,)),
            dma((nh,)), dma((nh, nrows * group)), dma((nh,)), dma((nh,)),
            dma((nh,)), dma((nh, nrows // 2)),
            dma((nh,)), dma((nh,)), dma((nh,)), dma((nh, 3)), dma((nh,)), dma((nh,)),
        ],
        compiler_params=pltpu.CompilerParams(
            collective_id=0, has_side_effects=True, vmem_limit_bytes=limit),
    )(*(pltpu.with_memory_space_constraint(v, pltpu.HBM) for v in (matrix, panel, factor)))
    return pl.pallas_call(
        functools.partial(hand_out, tile),
        out_shape=(jax.ShapeDtypeStruct(matrix.shape, F32), jax.ShapeDtypeStruct(panel.shape, F32)),
        in_specs=[vmem] * 6,
        out_specs=(hbm, hbm),
        scratch_shapes=[pltpu.VMEM((total, wide), F32), dma((tiles + 1,))],
        compiler_params=pltpu.CompilerParams(vmem_limit_bytes=8 * total * wide * 4 + (4 << 20)),
    )(*held)


def solution(mesh):
    in_specs = (P("row", "col"), P(("row", "col"), None), P())
    out_specs = (P("row", "col"), P(("row", "col"), None))
    return jax.shard_map(
        functools.partial(per_device, mesh.shape["row"], mesh.shape["col"]),
        mesh=mesh, in_specs=in_specs, out_specs=out_specs, check_vma=False)
```

```python
import functools

import jax
import jax.numpy as jnp
from jax import lax
from jax.experimental import pallas as pl
from jax.experimental.pallas import tpu as pltpu
from jax.sharding import PartitionSpec as P

F32 = jnp.float32
BF16 = jnp.bfloat16
NN = (((1,), (0,)), ((), ()))
NT = (((1,), (1,)), ((), ()))


def split(x):
    high = x.astype(BF16)
    return high, (x - high.astype(F32)).astype(BF16)


def mult(a, b, dims=NN):
    dot = functools.partial(lax.dot_general, dimension_numbers=dims, preferred_element_type=F32)
    return dot(a[0], b[1]) + dot(a[1], b[0]) + dot(a[0], b[0])


def wide_of(ref, span):
    return jnp.concatenate([ref[0, span, :], ref[1, span, :]], axis=1)


def tile_loop(count, body):
    if count <= 2:
        for i in range(count):
            body(i)
    else:
        pl.loop(0, count)(body)


def kernel(nrows, ncols, tile, a_hbm, panel_hbm, t_hbm, out_ref, corr_ref, v_hi, v_lo, y_hi, y_lo,
           a_ref, t_ref, vr, vc, sr, sc, q, qin, kpart, kin, kpair, kside, kfull,
           lpart, lin, lpair, lfull,
           at_hi, at_lo, vt_hi, vt_lo,
           local_sem, v_send, v_recv, vf_recv, q_send, q_recv, s_recv, sf_recv, sc_send, sc_recv,
           vc_send, vc_recv, k_send, k_recv, kg_recv):
    r, c = lax.axis_index("row"), lax.axis_index("col")
    lines = ncols // 2
    group = ncols // (2 * nrows)
    z, y = c // 2, c % 2
    total = a_ref.shape[0]
    nh, wide, hw = sc.shape
    blk, width = panel_hbm.shape
    tiles = total // tile
    mate = r + 1 - 2 * (r % 2)

    def rows(index, size):
        return pl.ds(pl.multiple_of(index * size, size), size)

    def peer(d):
        line = z
        for b in range(lines.bit_length()):
            if d >> b & 1:
                line = line + (1 << b) - (2 << b) * (z // (1 << b) % 2)
        return line

    def copy(src, dst, send, recv, row, col):
        return pltpu.make_async_remote_copy(
            src_ref=src, dst_ref=dst, send_sem=send, recv_sem=recv,
            device_id=(row, col), device_id_type=pl.DeviceIdType.MESH)

    def go(desc, when=None):
        if when is None:
            desc.start()
        else:
            pl.when(when)(desc.start)

    def sent(ref, sem):
        copy(ref, ref, sem, kg_recv.at[0], r, c).wait_send()

    def landed(ref, sem):
        copy(ref, ref, k_send.at[0], sem, r, c).wait_recv()

    def some(ref, h, count):
        return ref.at[h, pl.ds(0, count * blk), :]

    loads = [pltpu.make_async_copy(panel_hbm.at[:, pl.ds(h * hw, hw)], vr.at[h, rows(c, blk), :], local_sem.at[h])
             for h in range(nh)]
    loads.append(pltpu.make_async_copy(a_hbm, a_ref, local_sem.at[nh]))
    loads.append(pltpu.make_async_copy(t_hbm, t_ref, local_sem.at[nh + 1]))
    for load in loads[:nh]:
        load.start()

    across = z * 2 + 1 - y
    target = z // group
    barrier = pltpu.get_barrier_semaphore()

    def greet(row, col):
        pl.semaphore_signal(barrier, inc=1, device_id=(row, col), device_id_type=pl.DeviceIdType.MESH)

    for d in reversed(range(1, lines)):
        greet(r, peer(d) * 2 + y)
    greet(r, across)
    for d in range(1, nrows):
        greet(lax.rem(r + d, nrows), c)
    for load in loads[nh:]:
        load.start()
    for h in range(nh):
        loads[h].wait()
    pl.semaphore_wait(barrier, lines + nrows - 1)

    order = list(range(1, lines))
    for h in range(nh):
        own = vr.at[h, rows(c, blk), :]
        go(copy(own, own, v_send.at[0], v_recv.at[h, z], r, across))
        for d in order:
            go(copy(own, own, v_send.at[0], v_recv.at[h, z], r, peer(d) * 2 + y))

    loads[nh].wait()

    def flip(i):
        high, low = split(a_ref[pl.ds(pl.multiple_of(i * tile, tile), tile), :].T)
        at_hi[i] = high
        at_lo[i] = low
    tile_loop(tiles, flip)
    loads[nh + 1].wait()
    t_two = split(t_ref[...])
    tt_two = split(t_ref[...].T)

    for h in range(nh):
        for d in range(1, lines):
            line = peer(d)
            slot = vr.at[h, rows(line * 2 + y, blk), :]
            landed(slot, v_recv.at[h, line])
            go(copy(slot, slot, v_send.at[0], vf_recv.at[h, d // 2], r, across))

    holder = c * nrows // ncols
    first_block = lax.rem(c * nrows, ncols)
    same = r % 2 == holder % 2

    def hand_panel(h):
        held = vr.at[h, rows(first_block // nrows, wide), :]
        kept = vc.at[h]
        for d in range(1, nrows // 2):
            go(copy(held, kept, vc_send.at[0], vc_recv.at[h], lax.rem(r + 2 * d, nrows), c), r == holder)
        go(copy(held, kept, vc_send.at[0], vc_recv.at[h], mate, c), r == holder)

        @pl.when(r == holder)
        def _():
            kept[...] = held[...]

    def pass_panel(h):
        kept = vc.at[h]

        @pl.when(r != holder)
        def _():
            landed(kept, vc_recv.at[h])
        go(copy(kept, kept, vc_send.at[0], vc_recv.at[h], mate, c), (r != holder) & same)

    def reduce_product(h):
        for e in range(tiles):
            if e == 0:
                landed(some(vr, h, 1), v_recv.at[h, z])
            landed(some(vr, h, 2 if e else 1), vf_recv.at[h, e])
            i = peer(2 * e) // 2
            part = mult((at_hi[i], at_lo[i]), split(vr[h, rows(i, tile), :]))
            q[h] = part if e == 0 else q[h] + part
        for d in range(1, nrows):
            other = lax.rem(r + d, nrows)
            go(copy(q.at[h, rows(other, blk), :], qin.at[h, d], q_send.at[0], q_recv.at[h], other, c))

    reduce_product(0)
    hand_panel(0)
    reduce_product(1)

    def turn(i):
        span = pl.ds(pl.multiple_of(i * tile, tile), tile)
        v_two = split(wide_of(vr, span))
        v_hi[span, :], v_lo[span, :] = v_two
        high, low = split(mult(tt_two, v_two, NT))
        vt_hi[i] = high
        vt_lo[i] = low
    tile_loop(tiles, turn)

    place = lax.rem(c * nrows + r, ncols)
    here = r * group + lax.rem(z, group)
    products = []
    for h in range(nh):
        landed(qin.at[h, pl.ds(1, nrows - 1)], q_recv.at[h])
        product = q[h, rows(r, blk), :]
        for d in range(1, nrows):
            product = product + qin[h, d]
        products.append(split(product))
        scaled = None
        for g in range(h + 1):
            block = tuple(t[g * hw:(g + 1) * hw, h * hw:(h + 1) * hw] for t in t_two)
            term = mult(products[g], block)
            scaled = term if scaled is None else scaled + term
        mine = sc.at[h, rows(r, blk), :]
        mine[...] = scaled
        slot = sr.at[h, rows(place, blk), :]
        for d in [1] + order[:0:-1]:
            go(copy(mine, slot, q_send.at[0], s_recv.at[h, here], target, peer(d) * 2 + y))
        for d in range(1, nrows // 2):
            go(copy(mine, mine, sc_send.at[0], sc_recv.at[h, d], lax.rem(r + 2 * d, nrows), c))
        go(copy(mine, mine, sc_send.at[0], sc_recv.at[h, 0], mate, c))

    def from_mate(h):
        landed(some(sc, h, nrows // 2), sc_recv.at[h, 0])

    def forward_scaled(h):
        for d in range(1, nrows // 2):
            slot = sc.at[h, rows(lax.rem(r - 2 * d + nrows, nrows), blk), :]
            landed(slot, sc_recv.at[h, d])
            go(copy(slot, slot, sc_send.at[0], sc_recv.at[h, 0], mate, c))
        pl.when(target == r)(functools.partial(from_mate, h))
        for g in range(group):
            line = r * group + g
            for d in range(nrows):
                j = lax.rem(r + d, nrows)
                at = j * group + g
                slot = sr.at[h, rows(lax.rem((line * 2 + y) * nrows + j, ncols), blk), :]
                held = sc.at[h, rows(j, blk), :]
                straight = copy(held, slot, sc_send.at[0], sf_recv.at[h], r, across)
                passed = copy(slot, slot, sc_send.at[0], sf_recv.at[h], r, across)

                @pl.when(z == line)
                def _():
                    straight.start()
                    slot[...] = held[...]

                @pl.when(z != line)
                def _():
                    landed(slot, s_recv.at[h, at])
                    passed.start()

    def gather_scaled(h):
        landed(some(sr, h, nrows * group), sf_recv.at[h])

    def small(h, part, base):
        part[...] = jnp.zeros_like(part)
        for g in range(group):
            start = lax.rem(((r * group + g) * 2 + y) * nrows, ncols) * blk // tile
            for i in range(nrows * blk // tile):
                at = start + i
                part[...] += mult((vt_hi[at, base:, :], vt_lo[at, base:, :]), split(sr[h, rows(at, tile), :]))

    def pair_up(h, part, room, pair):
        size = pair.shape[0]
        go(copy(part.at[rows(mate % 2, size), :], room.at[0], k_send.at[0], k_recv.at[h, 0], mate, c))
        landed(room.at[0], k_recv.at[h, 0])
        pair[...] = part[rows(r % 2, size), :] + room[0]

    def spread(h, step, room, pair, slots):
        for i in slots:
            row, col = lax.rem(r + i // 2 * 2, nrows), across if i % 2 else c
            go(copy(pair, room.at[i], k_send.at[0], k_recv.at[h, step], row, col))

    def collect(h, step, room, pair, slots):
        landed(room.at[pl.ds(0, len(slots))], k_recv.at[h, step])
        summed = pair[...]
        for i in slots:
            summed = summed + room[i]
        return summed

    def finish_half(h, full, summed):
        mine = full.at[rows(r % 2, summed.shape[0]), :]
        mine[...] = summed
        go(copy(mine, mine, k_send.at[0], kg_recv.at[0], mate, c))


    hand_panel(1)
    forward_scaled(0)
    small(0, kpart, 0)
    pair_up(0, kpart, kin, kpair)
    spread(0, 1, kin, kpair, range(2, nrows, 2))
    forward_scaled(1)
    small(1, lpart, hw)
    pair_up(1, lpart, lin, lpair)
    spread(1, 1, lin, lpair, range(1, nrows))
    pass_panel(0)
    sent(vr.at[:, pl.ds(0, (2 * lines - 1) * blk), :], v_send.at[0])
    sent(sr.at[:, pl.ds(0, (nrows + lines - 2) * blk), :], q_send.at[0])
    kside[...] = collect(0, 1, kin, kpair, range(2, nrows, 2))
    spread(0, 2, kin, kside, (1,))
    gather_scaled(0)

    pass_panel(1)
    gather_scaled(1)

    everything = pl.ds(0, wide)
    vc_two = split(wide_of(vc, everything))

    def first(i):
        span = pl.ds(pl.multiple_of(i * tile, tile), tile)
        out_ref[span, :] = a_ref[span, :] - mult(split(wide_of(sr, span)), vc_two, NT)
    tile_loop(tiles, first)

    finish_half(1, lfull, collect(1, 1, lin, lpair, range(1, nrows)))
    finish_half(0, kfull, collect(0, 2, kin, kside, (1,)))
    for h in range(nh):
        pl.when(target != r)(functools.partial(from_mate, h))
    landed(vr.at[0, pl.ds(0, kpair.shape[0] + lpair.shape[0]), :], kg_recv.at[0])
    left = kfull[...]
    right = jnp.concatenate([left[hw:, :].T, lfull[...]], axis=0)
    k_two = split(jnp.concatenate([left, right], axis=1))
    y_hi[...], y_lo[...] = split(wide_of(sc, everything) - mult(vc_two, k_two))
    mine = rows(c, blk)
    corr_ref[...] = wide_of(sr, mine) - 0.5 * mult((v_hi[mine, :], v_lo[mine, :]), k_two)
    sent(sr.at[:, pl.ds(0, (nrows - 1 + nrows * group) * blk), :], sc_send.at[0])

    @pl.when(r == holder)
    def _():
        sent(vr.at[:, pl.ds(0, nrows // 2 * wide), :], vc_send.at[0])

    @pl.when((r != holder) & same)
    def _():
        sent(vc, vc_send.at[0])
    moved = (nrows // 2 + 2) * kpair.shape[0] + (nrows + 1) * lpair.shape[0]
    sent(vr.at[:, pl.ds(0, moved // nh), :], k_send.at[0])


def hand_out(tile, held_ref, held_corr_ref, v_hi, v_lo, y_hi, y_lo, out_hbm, corr_hbm, stage, sem):
    tiles = held_ref.shape[0] // tile
    copies = [pltpu.make_async_copy(held_corr_ref, corr_hbm, sem.at[tiles])]
    copies[0].start()
    for i in range(tiles):
        span = pl.ds(i * tile, tile)
        stage[span, :] = held_ref[span, :] - mult((v_hi[span, :], v_lo[span, :]), (y_hi[...], y_lo[...]), NT)
        copies.append(pltpu.make_async_copy(stage.at[span, :], out_hbm.at[span, :], sem.at[i]))
        copies[-1].start()
    for copy in copies:
        copy.wait()


def per_device(nrows, ncols, matrix, panel, factor):
    total, wide = matrix.shape
    blk, width = panel.shape
    tile = 4 * blk
    tiles = total // tile
    group = ncols // (2 * nrows)
    lines = ncols // 2
    nh = 2
    hw = width // nh
    dma = pltpu.SemaphoreType.DMA
    vmem = pl.BlockSpec(memory_space=pltpu.VMEM)
    hbm = pl.BlockSpec(memory_space=pltpu.HBM)
    limit = 4 * (5 * total * wide + 4 * total * width + 4 * wide * width + 16 * width * width) + (8 << 20)
    held = pl.pallas_call(
        functools.partial(kernel, nrows, ncols, tile),
        out_shape=(jax.ShapeDtypeStruct(matrix.shape, F32), jax.ShapeDtypeStruct(panel.shape, F32),
                   jax.ShapeDtypeStruct((total, width), BF16), jax.ShapeDtypeStruct((total, width), BF16),
                   jax.ShapeDtypeStruct((wide, width), BF16), jax.ShapeDtypeStruct((wide, width), BF16)),
        in_specs=[hbm] * 3,
        out_specs=(vmem,) * 6,
        scratch_shapes=[
            pltpu.VMEM((total, wide), F32),
            pltpu.VMEM((width, width), F32),
            pltpu.VMEM((nh, total, hw), F32),
            pltpu.VMEM((nh, wide, hw), F32),
            pltpu.VMEM((nh, total, hw), F32),
            pltpu.VMEM((nh, wide, hw), F32),
            pltpu.VMEM((nh, wide, hw), F32),
            pltpu.VMEM((nh, nrows, blk, hw), F32),
            pltpu.VMEM((width, hw), F32),
            pltpu.VMEM((nrows, width // 2, hw), F32),
            pltpu.VMEM((width // 2, hw), F32),
            pltpu.VMEM((width // 2, hw), F32),
            pltpu.VMEM((width, hw), F32),
            pltpu.VMEM((hw, hw), F32),
            pltpu.VMEM((nrows, hw // 2, hw), F32),
            pltpu.VMEM((hw // 2, hw), F32),
            pltpu.VMEM((hw, hw), F32),
            pltpu.VMEM((tiles, wide, tile), BF16),
            pltpu.VMEM((tiles, wide, tile), BF16),
            pltpu.VMEM((tiles, width, tile), BF16),
            pltpu.VMEM((tiles, width, tile), BF16),
            dma((nh + 2,)),
            dma((1,)), dma((nh, lines)), dma((nh, lines // 2)),
            dma((1,)), dma((nh,)), dma((nh, nrows * group)), dma((nh,)),
            dma((1,)), dma((nh, nrows // 2)),
            dma((1,)), dma((nh,)), dma((1,)), dma((nh, 3)), dma((1,)),
        ],
        compiler_params=pltpu.CompilerParams(
            collective_id=0, has_side_effects=True, vmem_limit_bytes=limit),
    )(*(pltpu.with_memory_space_constraint(v, pltpu.HBM) for v in (matrix, panel, factor)))
    return pl.pallas_call(
        functools.partial(hand_out, tile),
        out_shape=(jax.ShapeDtypeStruct(matrix.shape, F32), jax.ShapeDtypeStruct(panel.shape, F32)),
        in_specs=[vmem] * 6,
        out_specs=(hbm, hbm),
        scratch_shapes=[pltpu.VMEM((total, wide), F32), dma((tiles + 1,))],
        compiler_params=pltpu.CompilerParams(vmem_limit_bytes=8 * total * wide * 4 + (4 << 20)),
    )(*held)


def solution(mesh):
    in_specs = (P("row", "col"), P(("row", "col"), None), P())
    out_specs = (P("row", "col"), P(("row", "col"), None))
    return jax.shard_map(
        functools.partial(per_device, mesh.shape["row"], mesh.shape["col"]),
        mesh=mesh, in_specs=in_specs, out_specs=out_specs, check_vma=False)
```

```python
import functools

import jax
import jax.numpy as jnp
from jax import lax
from jax.experimental import pallas as pl
from jax.experimental.pallas import tpu as pltpu
from jax.sharding import PartitionSpec as P

F32 = jnp.float32
BF16 = jnp.bfloat16
NN = (((1,), (0,)), ((), ()))
NT = (((1,), (1,)), ((), ()))


def split(x):
    high = x.astype(BF16)
    return high, (x - high.astype(F32)).astype(BF16)


def mult(a, b, dims=NN):
    dot = functools.partial(lax.dot_general, dimension_numbers=dims, preferred_element_type=F32)
    return dot(a[0], b[1]) + dot(a[1], b[0]) + dot(a[0], b[0])


def wide_of(ref, span):
    return jnp.concatenate([ref[0, span, :], ref[1, span, :]], axis=1)


def tile_loop(count, body):
    if count <= 2:
        for i in range(count):
            body(i)
    else:
        pl.loop(0, count)(body)


def kernel(nrows, ncols, tile, a_hbm, panel_hbm, t_hbm, out_ref, corr_ref, v_hi, v_lo, y_hi, y_lo,
           a_ref, t_ref, vr, vc, sr, sc, q, qin, kpart, kin, kpair, kside, kfull,
           lpart, lin, lpair, lfull,
           at_hi, at_lo, vt_hi, vt_lo,
           local_sem, v_send, v_recv, vf_recv, q_send, q_recv, s_recv, sf_recv, sc_send, sc_recv,
           vc_send, vc_recv, k_send, k_recv, kg_recv):
    r, c = lax.axis_index("row"), lax.axis_index("col")
    lines = ncols // 2
    group = ncols // (2 * nrows)
    z, y = c // 2, c % 2
    total = a_ref.shape[0]
    nh, wide, hw = sc.shape
    blk, width = panel_hbm.shape
    tiles = total // tile
    mate = r + 1 - 2 * (r % 2)

    def rows(index, size):
        return pl.ds(pl.multiple_of(index * size, size), size)

    def peer(d):
        line = z
        for b in range(lines.bit_length()):
            if d >> b & 1:
                line = line + (1 << b) - (2 << b) * (z // (1 << b) % 2)
        return line

    def copy(src, dst, send, recv, row, col):
        return pltpu.make_async_remote_copy(
            src_ref=src, dst_ref=dst, send_sem=send, recv_sem=recv,
            device_id=(row, col), device_id_type=pl.DeviceIdType.MESH)

    def go(desc, when=None):
        if when is None:
            desc.start()
        else:
            pl.when(when)(desc.start)

    def sent(ref, sem):
        copy(ref, ref, sem, kg_recv.at[0], r, c).wait_send()

    def landed(ref, sem):
        copy(ref, ref, k_send.at[0], sem, r, c).wait_recv()

    def some(ref, h, count):
        return ref.at[h, pl.ds(0, count * blk), :]

    loads = [pltpu.make_async_copy(panel_hbm.at[:, pl.ds(h * hw, hw)], vr.at[h, rows(c, blk), :], local_sem.at[h])
             for h in range(nh)]
    loads.append(pltpu.make_async_copy(a_hbm, a_ref, local_sem.at[nh]))
    loads.append(pltpu.make_async_copy(t_hbm, t_ref, local_sem.at[nh + 1]))
    for load in loads[:nh]:
        load.start()

    across = z * 2 + 1 - y
    target = z // group
    barrier = pltpu.get_barrier_semaphore()

    def greet(row, col):
        pl.semaphore_signal(barrier, inc=1, device_id=(row, col), device_id_type=pl.DeviceIdType.MESH)

    for d in reversed(range(1, lines)):
        greet(r, peer(d) * 2 + y)
    greet(r, across)
    for d in range(1, nrows):
        greet(lax.rem(r + d, nrows), c)
    for load in loads[nh:]:
        load.start()
    for h in range(nh):
        loads[h].wait()
    pl.semaphore_wait(barrier, lines + nrows - 1)

    order = list(range(1, lines))
    for h in range(nh):
        own = vr.at[h, rows(c, blk), :]
        go(copy(own, own, v_send.at[0], v_recv.at[h, z], r, across))
        for d in order:
            go(copy(own, own, v_send.at[0], v_recv.at[h, z], r, peer(d) * 2 + y))

    loads[nh].wait()

    def flip(i):
        high, low = split(a_ref[pl.ds(pl.multiple_of(i * tile, tile), tile), :].T)
        at_hi[i] = high
        at_lo[i] = low
    tile_loop(tiles, flip)
    loads[nh + 1].wait()
    t_two = split(t_ref[...])
    tt_two = split(t_ref[...].T)

    for h in range(nh):
        for d in range(1, lines):
            line = peer(d)
            slot = vr.at[h, rows(line * 2 + y, blk), :]
            landed(slot, v_recv.at[h, line])
            go(copy(slot, slot, v_send.at[0], vf_recv.at[h, d // 2], r, across))

    holder = c * nrows // ncols
    first_block = lax.rem(c * nrows, ncols)
    same = r % 2 == holder % 2

    def hand_panel(h):
        held = vr.at[h, rows(first_block // nrows, wide), :]
        kept = vc.at[h]
        for d in range(1, nrows // 2):
            go(copy(held, kept, vc_send.at[0], vc_recv.at[h], lax.rem(r + 2 * d, nrows), c), r == holder)
        go(copy(held, kept, vc_send.at[0], vc_recv.at[h], mate, c), r == holder)

        @pl.when(r == holder)
        def _():
            kept[...] = held[...]

    def pass_panel(h):
        kept = vc.at[h]

        @pl.when(r != holder)
        def _():
            landed(kept, vc_recv.at[h])
        go(copy(kept, kept, vc_send.at[0], vc_recv.at[h], mate, c), (r != holder) & same)

    def reduce_product(h):
        for e in range(tiles):
            if e == 0:
                landed(some(vr, h, 1), v_recv.at[h, z])
            landed(some(vr, h, 2 if e else 1), vf_recv.at[h, e])
            i = peer(2 * e) // 2
            part = mult((at_hi[i], at_lo[i]), split(vr[h, rows(i, tile), :]))
            q[h] = part if e == 0 else q[h] + part
        for d in range(1, nrows):
            other = lax.rem(r + d, nrows)
            go(copy(q.at[h, rows(other, blk), :], qin.at[h, d], q_send.at[0], q_recv.at[h], other, c))

    reduce_product(0)
    hand_panel(0)
    reduce_product(1)

    def turn(i):
        span = pl.ds(pl.multiple_of(i * tile, tile), tile)
        v_two = split(wide_of(vr, span))
        v_hi[span, :], v_lo[span, :] = v_two
        high, low = split(mult(tt_two, v_two, NT))
        vt_hi[i] = high
        vt_lo[i] = low

    place = lax.rem(c * nrows + r, ncols)
    here = r * group + lax.rem(z, group)
    products = []
    for h in range(nh):
        landed(qin.at[h, pl.ds(1, nrows - 1)], q_recv.at[h])
        product = q[h, rows(r, blk), :]
        for d in range(1, nrows):
            product = product + qin[h, d]
        products.append(split(product))
        scaled = None
        for g in range(h + 1):
            block = tuple(t[g * hw:(g + 1) * hw, h * hw:(h + 1) * hw] for t in t_two)
            term = mult(products[g], block)
            scaled = term if scaled is None else scaled + term
        mine = sc.at[h, rows(r, blk), :]
        mine[...] = scaled
        slot = sr.at[h, rows(place, blk), :]
        for d in [1] + order[:0:-1]:
            go(copy(mine, slot, q_send.at[0], s_recv.at[h, here], target, peer(d) * 2 + y))
        for d in range(1, nrows // 2):
            go(copy(mine, mine, sc_send.at[0], sc_recv.at[h, d], lax.rem(r + 2 * d, nrows), c))
        go(copy(mine, mine, sc_send.at[0], sc_recv.at[h, 0], mate, c))
        if h == 0:
            hand_panel(1)
            tile_loop(tiles, turn)

    def from_mate(h):
        landed(some(sc, h, nrows // 2), sc_recv.at[h, 0])

    def hand_on(h):
        for d in range(1, nrows // 2):
            slot = sc.at[h, rows(lax.rem(r - 2 * d + nrows, nrows), blk), :]
            landed(slot, sc_recv.at[h, d])
            go(copy(slot, slot, sc_send.at[0], sc_recv.at[h, 0], mate, c))

    def forward_scaled(h):
        pl.when(target // 2 == r // 2)(functools.partial(hand_on, h))
        pl.when(target == r)(functools.partial(from_mate, h))
        for g in range(group):
            line = r * group + g
            for d in range(nrows):
                j = lax.rem((mate if d % 2 else r) + d // 2 * 2, nrows)
                at = j * group + g
                slot = sr.at[h, rows(lax.rem((line * 2 + y) * nrows + j, ncols), blk), :]
                held = sc.at[h, rows(j, blk), :]
                straight = copy(held, slot, sc_send.at[0], sf_recv.at[h], r, across)
                passed = copy(slot, slot, sc_send.at[0], sf_recv.at[h], r, across)

                @pl.when(z == line)
                def _():
                    straight.start()
                    slot[...] = held[...]

                @pl.when(z != line)
                def _():
                    landed(slot, s_recv.at[h, at])
                    passed.start()


    def gather_scaled(h):
        landed(some(sr, h, nrows * group), sf_recv.at[h])

    def small(h, part, base):
        part[...] = jnp.zeros_like(part)
        for g in range(group):
            start = lax.rem(((r * group + g) * 2 + y) * nrows, ncols) * blk // tile
            for i in range(nrows * blk // tile):
                at = start + i
                part[...] += mult((vt_hi[at, base:, :], vt_lo[at, base:, :]), split(sr[h, rows(at, tile), :]))

    def pair_up(h, part, room, pair):
        size = pair.shape[0]
        go(copy(part.at[rows(mate % 2, size), :], room.at[0], k_send.at[0], k_recv.at[h, 0], mate, c))
        landed(room.at[0], k_recv.at[h, 0])
        pair[...] = part[rows(r % 2, size), :] + room[0]

    def spread(h, step, room, pair, slots):
        for i in slots:
            row, col = lax.rem(r + i // 2 * 2, nrows), across if i % 2 else c
            go(copy(pair, room.at[i], k_send.at[0], k_recv.at[h, step], row, col))

    def collect(h, step, room, pair, slots):
        landed(room.at[pl.ds(0, len(slots))], k_recv.at[h, step])
        summed = pair[...]
        for i in slots:
            summed = summed + room[i]
        return summed

    def finish_half(h, full, summed):
        mine = full.at[rows(r % 2, summed.shape[0]), :]
        mine[...] = summed
        go(copy(mine, mine, k_send.at[0], kg_recv.at[0], mate, c))


    forward_scaled(0)
    small(0, kpart, 0)
    pair_up(0, kpart, kin, kpair)
    spread(0, 1, kin, kpair, range(2, nrows, 2))
    forward_scaled(1)
    small(1, lpart, hw)
    pair_up(1, lpart, lin, lpair)
    spread(1, 1, lin, lpair, range(1, nrows))
    for h in range(nh):
        pl.when(target // 2 != r // 2)(functools.partial(hand_on, h))
    pass_panel(0)
    sent(vr.at[:, pl.ds(0, (2 * lines - 1) * blk), :], v_send.at[0])
    sent(sr.at[:, pl.ds(0, (nrows + lines - 2) * blk), :], q_send.at[0])
    kside[...] = collect(0, 1, kin, kpair, range(2, nrows, 2))
    spread(0, 2, kin, kside, (1,))
    gather_scaled(0)
    pass_panel(1)
    for h in range(nh):
        pl.when(target != r)(functools.partial(from_mate, h))
    everything = pl.ds(0, wide)
    sc_turned = wide_of(sc, everything).T
    vc_turned = split(wide_of(vc, everything).T)
    vc_near, vc_rest = (tuple(v[h * hw:(h + 1) * hw, :] for v in vc_turned) for h in range(nh))

    def first(i):
        span = pl.ds(pl.multiple_of(i * tile, tile), tile)
        out_ref[span, :] = a_ref[span, :] - mult(split(sr[0, span, :]), vc_near)
    tile_loop(tiles, first)

    def second(i):
        span = pl.ds(pl.multiple_of(i * tile, tile), tile)
        out_ref[span, :] = out_ref[span, :] - mult(split(sr[1, span, :]), vc_rest)
    finish_half(1, lfull, collect(1, 1, lin, lpair, range(1, nrows)))
    finish_half(0, kfull, collect(0, 2, kin, kside, (1,)))
    gather_scaled(1)
    tile_loop(tiles, second)
    landed(vr.at[0, pl.ds(0, kpair.shape[0] + lpair.shape[0]), :], kg_recv.at[0])
    left = kfull[...]
    right = jnp.concatenate([left[hw:, :].T, lfull[...]], axis=0)
    k_two = split(jnp.concatenate([left, right], axis=1))
    y_hi[...], y_lo[...] = split(sc_turned - mult(k_two, vc_turned))
    mine = rows(c, blk)
    corr_ref[...] = wide_of(sr, mine) - 0.5 * mult((v_hi[mine, :], v_lo[mine, :]), k_two)
    sent(sr.at[:, pl.ds(0, (nrows - 1 + nrows * group) * blk), :], sc_send.at[0])

    @pl.when(r == holder)
    def _():
        sent(vr.at[:, pl.ds(0, nrows // 2 * wide), :], vc_send.at[0])

    @pl.when((r != holder) & same)
    def _():
        sent(vc, vc_send.at[0])
    moved = (nrows // 2 + 2) * kpair.shape[0] + (nrows + 1) * lpair.shape[0]
    sent(vr.at[:, pl.ds(0, moved // nh), :], k_send.at[0])


def hand_out(tile, held_ref, held_corr_ref, v_hi, v_lo, y_hi, y_lo, out_hbm, corr_hbm, stage, sem):
    tiles = held_ref.shape[0] // tile
    copies = [pltpu.make_async_copy(held_corr_ref, corr_hbm, sem.at[tiles])]
    copies[0].start()
    for i in range(tiles):
        span = pl.ds(i * tile, tile)
        stage[span, :] = held_ref[span, :] - mult((v_hi[span, :], v_lo[span, :]), (y_hi[...], y_lo[...]))
        copies.append(pltpu.make_async_copy(stage.at[span, :], out_hbm.at[span, :], sem.at[i]))
        copies[-1].start()
    for copy in copies:
        copy.wait()


def per_device(nrows, ncols, matrix, panel, factor):
    total, wide = matrix.shape
    blk, width = panel.shape
    tile = 4 * blk
    tiles = total // tile
    group = ncols // (2 * nrows)
    lines = ncols // 2
    nh = 2
    hw = width // nh
    dma = pltpu.SemaphoreType.DMA
    vmem = pl.BlockSpec(memory_space=pltpu.VMEM)
    hbm = pl.BlockSpec(memory_space=pltpu.HBM)
    limit = 4 * (5 * total * wide + 4 * total * width + 4 * wide * width + 16 * width * width) + (8 << 20)
    held = pl.pallas_call(
        functools.partial(kernel, nrows, ncols, tile),
        out_shape=(jax.ShapeDtypeStruct(matrix.shape, F32), jax.ShapeDtypeStruct(panel.shape, F32),
                   jax.ShapeDtypeStruct((total, width), BF16), jax.ShapeDtypeStruct((total, width), BF16),
                   jax.ShapeDtypeStruct((width, wide), BF16), jax.ShapeDtypeStruct((width, wide), BF16)),
        in_specs=[hbm] * 3,
        out_specs=(vmem,) * 6,
        scratch_shapes=[
            pltpu.VMEM((total, wide), F32),
            pltpu.VMEM((width, width), F32),
            pltpu.VMEM((nh, total, hw), F32),
            pltpu.VMEM((nh, wide, hw), F32),
            pltpu.VMEM((nh, total, hw), F32),
            pltpu.VMEM((nh, wide, hw), F32),
            pltpu.VMEM((nh, wide, hw), F32),
            pltpu.VMEM((nh, nrows, blk, hw), F32),
            pltpu.VMEM((width, hw), F32),
            pltpu.VMEM((nrows, width // 2, hw), F32),
            pltpu.VMEM((width // 2, hw), F32),
            pltpu.VMEM((width // 2, hw), F32),
            pltpu.VMEM((width, hw), F32),
            pltpu.VMEM((hw, hw), F32),
            pltpu.VMEM((nrows, hw // 2, hw), F32),
            pltpu.VMEM((hw // 2, hw), F32),
            pltpu.VMEM((hw, hw), F32),
            pltpu.VMEM((tiles, wide, tile), BF16),
            pltpu.VMEM((tiles, wide, tile), BF16),
            pltpu.VMEM((tiles, width, tile), BF16),
            pltpu.VMEM((tiles, width, tile), BF16),
            dma((nh + 2,)),
            dma((1,)), dma((nh, lines)), dma((nh, lines // 2)),
            dma((1,)), dma((nh,)), dma((nh, nrows * group)), dma((nh,)),
            dma((1,)), dma((nh, nrows // 2)),
            dma((1,)), dma((nh,)), dma((1,)), dma((nh, 3)), dma((1,)),
        ],
        compiler_params=pltpu.CompilerParams(
            collective_id=0, has_side_effects=True, vmem_limit_bytes=limit),
    )(*(pltpu.with_memory_space_constraint(v, pltpu.HBM) for v in (matrix, panel, factor)))
    return pl.pallas_call(
        functools.partial(hand_out, tile),
        out_shape=(jax.ShapeDtypeStruct(matrix.shape, F32), jax.ShapeDtypeStruct(panel.shape, F32)),
        in_specs=[vmem] * 6,
        out_specs=(hbm, hbm),
        scratch_shapes=[pltpu.VMEM((total, wide), F32), dma((tiles + 1,))],
        compiler_params=pltpu.CompilerParams(vmem_limit_bytes=8 * total * wide * 4 + (4 << 20)),
    )(*held)


def solution(mesh):
    in_specs = (P("row", "col"), P(("row", "col"), None), P())
    out_specs = (P("row", "col"), P(("row", "col"), None))
    return jax.shard_map(
        functools.partial(per_device, mesh.shape["row"], mesh.shape["col"]),
        mesh=mesh, in_specs=in_specs, out_specs=out_specs, check_vma=False)
```

```python
import functools

import jax
import jax.numpy as jnp
from jax import lax
from jax.experimental import pallas as pl
from jax.experimental.pallas import tpu as pltpu
from jax.sharding import PartitionSpec as P

F32 = jnp.float32
BF16 = jnp.bfloat16
NN = (((1,), (0,)), ((), ()))
NT = (((1,), (1,)), ((), ()))


def split(x):
    high = x.astype(BF16)
    return high, (x - high.astype(F32)).astype(BF16)


def mult(a, b, dims=NN):
    dot = functools.partial(lax.dot_general, dimension_numbers=dims, preferred_element_type=F32)
    return dot(a[0], b[1]) + dot(a[1], b[0]) + dot(a[0], b[0])


def wide_of(ref, span):
    return jnp.concatenate([ref[0, span, :], ref[1, span, :]], axis=1)


def tile_loop(count, body):
    if count <= 2:
        for i in range(count):
            body(i)
    else:
        pl.loop(0, count)(body)


def kernel(nrows, ncols, tile, a_hbm, panel_hbm, t_hbm, out_ref, corr_ref, v_hi, v_lo, y_hi, y_lo,
           a_ref, t_ref, vr, vc, sr, sc, q, qin, kpart, kin, kpair, kside, kfull,
           lpart, lin, lpair, lfull,
           at_hi, at_lo, vt_hi, vt_lo,
           local_sem, v_send, v_recv, vf_recv, q_send, q_recv, s_recv, sf_recv, sc_send, sc_recv,
           vc_send, vc_recv, k_send, k_recv, kg_recv):
    r, c = lax.axis_index("row"), lax.axis_index("col")
    lines = ncols // 2
    group = ncols // (2 * nrows)
    z, y = c // 2, c % 2
    total = a_ref.shape[0]
    nh, wide, hw = sc.shape
    blk, width = panel_hbm.shape
    tiles = total // tile
    mate = r + 1 - 2 * (r % 2)

    def rows(index, size):
        return pl.ds(pl.multiple_of(index * size, size), size)

    def peer(d):
        line = z
        for b in range(lines.bit_length()):
            if d >> b & 1:
                line = line + (1 << b) - (2 << b) * (z // (1 << b) % 2)
        return line

    def copy(src, dst, send, recv, row, col):
        return pltpu.make_async_remote_copy(
            src_ref=src, dst_ref=dst, send_sem=send, recv_sem=recv,
            device_id=(row, col), device_id_type=pl.DeviceIdType.MESH)

    def go(desc, when=None):
        if when is None:
            desc.start()
        else:
            pl.when(when)(desc.start)

    def sent(ref, sem):
        copy(ref, ref, sem, kg_recv.at[0], r, c).wait_send()

    def landed(ref, sem):
        copy(ref, ref, k_send.at[0], sem, r, c).wait_recv()

    def some(ref, h, count):
        return ref.at[h, pl.ds(0, count * blk), :]

    loads = [pltpu.make_async_copy(panel_hbm.at[:, pl.ds(h * hw, hw)], vr.at[h, rows(c, blk), :], local_sem.at[h])
             for h in range(nh)]
    loads.append(pltpu.make_async_copy(a_hbm, a_ref, local_sem.at[nh]))
    loads.append(pltpu.make_async_copy(t_hbm, t_ref, local_sem.at[nh + 1]))
    for load in loads[:nh]:
        load.start()

    across = z * 2 + 1 - y
    target = z // group
    barrier = pltpu.get_barrier_semaphore()

    def greet(row, col):
        pl.semaphore_signal(barrier, inc=1, device_id=(row, col), device_id_type=pl.DeviceIdType.MESH)

    for d in reversed(range(1, lines)):
        greet(r, peer(d) * 2 + y)
    greet(r, across)
    for d in range(1, nrows):
        greet(lax.rem(r + d, nrows), c)
    for load in loads[nh:]:
        load.start()
    for h in range(nh):
        loads[h].wait()
    pl.semaphore_wait(barrier, lines + nrows - 1)

    order = list(range(1, lines))
    for h in range(nh):
        own = vr.at[h, rows(c, blk), :]
        go(copy(own, own, v_send.at[0], v_recv.at[h, z], r, across))
        for d in order:
            go(copy(own, own, v_send.at[0], v_recv.at[h, z], r, peer(d) * 2 + y))

    loads[nh].wait()

    def flip(i):
        high, low = split(a_ref[pl.ds(pl.multiple_of(i * tile, tile), tile), :].T)
        at_hi[i] = high
        at_lo[i] = low
    tile_loop(tiles, flip)
    loads[nh + 1].wait()
    t_two = split(t_ref[...])
    tt_two = split(t_ref[...].T)

    for h in range(nh):
        for d in range(1, lines):
            line = peer(d)
            slot = vr.at[h, rows(line * 2 + y, blk), :]
            landed(slot, v_recv.at[h, line])
            go(copy(slot, slot, v_send.at[0], vf_recv.at[h, d // 2], r, across))

    holder = c * nrows // ncols
    first_block = lax.rem(c * nrows, ncols)
    same = r % 2 == holder % 2

    def hand_panel(h):
        held = vr.at[h, rows(first_block // nrows, wide), :]
        kept = vc.at[h]
        for d in range(1, nrows // 2):
            go(copy(held, kept, vc_send.at[0], vc_recv.at[h], lax.rem(r + 2 * d, nrows), c), r == holder)
        go(copy(held, kept, vc_send.at[0], vc_recv.at[h], mate, c), r == holder)

        @pl.when(r == holder)
        def _():
            kept[...] = held[...]

    def pass_panel(h):
        kept = vc.at[h]

        @pl.when((r != holder) & same)
        def _():
            landed(kept, vc_recv.at[h])
            copy(kept, kept, vc_send.at[0], vc_recv.at[h], mate, c).start()

    def take_panel(h):
        pl.when(jnp.logical_not(same))(functools.partial(landed, vc.at[h], vc_recv.at[h]))

    def reduce_product(h):
        for e in range(tiles):
            if e == 0:
                landed(some(vr, h, 1), v_recv.at[h, z])
            landed(some(vr, h, 2 if e else 1), vf_recv.at[h, e])
            i = peer(2 * e) // 2
            part = mult((at_hi[i], at_lo[i]), split(vr[h, rows(i, tile), :]))
            q[h] = part if e == 0 else q[h] + part
        for d in range(1, nrows):
            other = lax.rem(r + d, nrows)
            go(copy(q.at[h, rows(other, blk), :], qin.at[h, d], q_send.at[0], q_recv.at[h], other, c))

    reduce_product(0)
    hand_panel(0)
    reduce_product(1)

    def turn(i):
        span = pl.ds(pl.multiple_of(i * tile, tile), tile)
        v_two = split(wide_of(vr, span))
        v_hi[span, :], v_lo[span, :] = v_two
        high, low = split(mult(tt_two, v_two, NT))
        vt_hi[i] = high
        vt_lo[i] = low

    place = lax.rem(c * nrows + r, ncols)
    here = r * group + lax.rem(z, group)
    products = []
    for h in range(nh):
        landed(qin.at[h, pl.ds(1, nrows - 1)], q_recv.at[h])
        product = q[h, rows(r, blk), :]
        for d in range(1, nrows):
            product = product + qin[h, d]
        products.append(split(product))
        scaled = None
        for g in range(h + 1):
            block = tuple(t[g * hw:(g + 1) * hw, h * hw:(h + 1) * hw] for t in t_two)
            term = mult(products[g], block)
            scaled = term if scaled is None else scaled + term
        mine = sc.at[h, rows(r, blk), :]
        mine[...] = scaled
        slot = sr.at[h, rows(place, blk), :]
        for d in [1] + order[:0:-1]:
            go(copy(mine, slot, q_send.at[0], s_recv.at[h, here], target, peer(d) * 2 + y))
        for d in range(1, nrows // 2):
            go(copy(mine, mine, sc_send.at[0], sc_recv.at[h, d], lax.rem(r + 2 * d, nrows), c))
        go(copy(mine, mine, sc_send.at[0], sc_recv.at[h, 0], mate, c))
        if h == 0:
            hand_panel(1)
            tile_loop(tiles, turn)

    def from_mate(h):
        landed(some(sc, h, nrows // 2), sc_recv.at[h, 0])

    def hand_on(h):
        for d in range(1, nrows // 2):
            slot = sc.at[h, rows(lax.rem(r - 2 * d + nrows, nrows), blk), :]
            landed(slot, sc_recv.at[h, d])
            go(copy(slot, slot, sc_send.at[0], sc_recv.at[h, 0], mate, c))

    def forward_scaled(h):
        pl.when(target // 2 == r // 2)(functools.partial(hand_on, h))
        pl.when(target == r)(functools.partial(from_mate, h))
        for g in range(group):
            line = r * group + g
            for d in range(nrows):
                j = lax.rem((mate if d % 2 else r) + d // 2 * 2, nrows)
                at = j * group + g
                slot = sr.at[h, rows(lax.rem((line * 2 + y) * nrows + j, ncols), blk), :]
                held = sc.at[h, rows(j, blk), :]
                straight = copy(held, slot, sc_send.at[0], sf_recv.at[h], r, across)
                passed = copy(slot, slot, sc_send.at[0], sf_recv.at[h], r, across)

                @pl.when(z == line)
                def _():
                    straight.start()
                    slot[...] = held[...]

                @pl.when(z != line)
                def _():
                    landed(slot, s_recv.at[h, at])
                    passed.start()


    def gather_scaled(h):
        landed(some(sr, h, nrows * group), sf_recv.at[h])

    def small(h, part, base):
        part[...] = jnp.zeros_like(part)
        for g in range(group):
            start = lax.rem(((r * group + g) * 2 + y) * nrows, ncols) * blk // tile
            for i in range(nrows * blk // tile):
                at = start + i
                part[...] += mult((vt_hi[at, base:, :], vt_lo[at, base:, :]), split(sr[h, rows(at, tile), :]))

    def pair_up(h, part, room, pair):
        size = pair.shape[0]
        go(copy(part.at[rows(mate % 2, size), :], room.at[0], k_send.at[0], k_recv.at[h, 0], mate, c))
        landed(room.at[0], k_recv.at[h, 0])
        pair[...] = part[rows(r % 2, size), :] + room[0]

    def spread(h, step, room, pair, slots):
        for i in slots:
            row, col = lax.rem(r + i // 2 * 2, nrows), across if i % 2 else c
            go(copy(pair, room.at[i], k_send.at[0], k_recv.at[h, step], row, col))

    def collect(h, step, room, pair, slots):
        landed(room.at[pl.ds(0, len(slots))], k_recv.at[h, step])
        summed = pair[...]
        for i in slots:
            summed = summed + room[i]
        return summed

    def finish_half(h, full, summed):
        mine = full.at[rows(r % 2, summed.shape[0]), :]
        mine[...] = summed
        go(copy(mine, mine, k_send.at[0], kg_recv.at[0], mate, c))


    forward_scaled(0)
    small(0, kpart, 0)
    pair_up(0, kpart, kin, kpair)
    spread(0, 1, kin, kpair, range(2, nrows, 2))
    forward_scaled(1)
    small(1, lpart, hw)
    pair_up(1, lpart, lin, lpair)
    spread(1, 1, lin, lpair, range(1, nrows))
    for h in range(nh):
        pl.when(target // 2 != r // 2)(functools.partial(hand_on, h))
    pass_panel(0)
    pass_panel(1)
    sent(vr.at[:, pl.ds(0, (2 * lines - 1) * blk), :], v_send.at[0])
    sent(sr.at[:, pl.ds(0, (nrows + lines - 2) * blk), :], q_send.at[0])
    kside[...] = collect(0, 1, kin, kpair, range(2, nrows, 2))
    spread(0, 2, kin, kside, (1,))
    gather_scaled(0)
    take_panel(0)
    take_panel(1)
    for h in range(nh):
        pl.when(target != r)(functools.partial(from_mate, h))
    everything = pl.ds(0, wide)
    sc_turned = wide_of(sc, everything).T
    vc_turned = split(wide_of(vc, everything).T)
    vc_near, vc_rest = (tuple(v[h * hw:(h + 1) * hw, :] for v in vc_turned) for h in range(nh))

    def first(i):
        span = pl.ds(pl.multiple_of(i * tile, tile), tile)
        out_ref[span, :] = a_ref[span, :] - mult(split(sr[0, span, :]), vc_near)
    tile_loop(tiles, first)

    def second(i):
        span = pl.ds(pl.multiple_of(i * tile, tile), tile)
        out_ref[span, :] = out_ref[span, :] - mult(split(sr[1, span, :]), vc_rest)
    finish_half(1, lfull, collect(1, 1, lin, lpair, range(1, nrows)))
    finish_half(0, kfull, collect(0, 2, kin, kside, (1,)))
    gather_scaled(1)
    tile_loop(tiles, second)
    landed(vr.at[0, pl.ds(0, kpair.shape[0] + lpair.shape[0]), :], kg_recv.at[0])
    left = kfull[...]
    right = jnp.concatenate([left[hw:, :].T, lfull[...]], axis=0)
    k_two = split(jnp.concatenate([left, right], axis=1))
    y_hi[...], y_lo[...] = split(sc_turned - mult(k_two, vc_turned))
    mine = rows(c, blk)
    corr_ref[...] = wide_of(sr, mine) - 0.5 * mult((v_hi[mine, :], v_lo[mine, :]), k_two)
    sent(sr.at[:, pl.ds(0, (nrows - 1 + nrows * group) * blk), :], sc_send.at[0])

    @pl.when(r == holder)
    def _():
        sent(vr.at[:, pl.ds(0, nrows // 2 * wide), :], vc_send.at[0])

    @pl.when((r != holder) & same)
    def _():
        sent(vc, vc_send.at[0])
    moved = (nrows // 2 + 2) * kpair.shape[0] + (nrows + 1) * lpair.shape[0]
    sent(vr.at[:, pl.ds(0, moved // nh), :], k_send.at[0])


def hand_out(tile, held_ref, held_corr_ref, v_hi, v_lo, y_hi, y_lo, out_hbm, corr_hbm, stage, sem):
    tiles = held_ref.shape[0] // tile
    copies = [pltpu.make_async_copy(held_corr_ref, corr_hbm, sem.at[tiles])]
    copies[0].start()
    for i in range(tiles):
        span = pl.ds(i * tile, tile)
        stage[span, :] = held_ref[span, :] - mult((v_hi[span, :], v_lo[span, :]), (y_hi[...], y_lo[...]))
        copies.append(pltpu.make_async_copy(stage.at[span, :], out_hbm.at[span, :], sem.at[i]))
        copies[-1].start()
    for copy in copies:
        copy.wait()


def per_device(nrows, ncols, matrix, panel, factor):
    total, wide = matrix.shape
    blk, width = panel.shape
    tile = 4 * blk
    tiles = total // tile
    group = ncols // (2 * nrows)
    lines = ncols // 2
    nh = 2
    hw = width // nh
    dma = pltpu.SemaphoreType.DMA
    vmem = pl.BlockSpec(memory_space=pltpu.VMEM)
    hbm = pl.BlockSpec(memory_space=pltpu.HBM)
    limit = 4 * (5 * total * wide + 4 * total * width + 4 * wide * width + 16 * width * width) + (8 << 20)
    held = pl.pallas_call(
        functools.partial(kernel, nrows, ncols, tile),
        out_shape=(jax.ShapeDtypeStruct(matrix.shape, F32), jax.ShapeDtypeStruct(panel.shape, F32),
                   jax.ShapeDtypeStruct((total, width), BF16), jax.ShapeDtypeStruct((total, width), BF16),
                   jax.ShapeDtypeStruct((width, wide), BF16), jax.ShapeDtypeStruct((width, wide), BF16)),
        in_specs=[hbm] * 3,
        out_specs=(vmem,) * 6,
        scratch_shapes=[
            pltpu.VMEM((total, wide), F32),
            pltpu.VMEM((width, width), F32),
            pltpu.VMEM((nh, total, hw), F32),
            pltpu.VMEM((nh, wide, hw), F32),
            pltpu.VMEM((nh, total, hw), F32),
            pltpu.VMEM((nh, wide, hw), F32),
            pltpu.VMEM((nh, wide, hw), F32),
            pltpu.VMEM((nh, nrows, blk, hw), F32),
            pltpu.VMEM((width, hw), F32),
            pltpu.VMEM((nrows, width // 2, hw), F32),
            pltpu.VMEM((width // 2, hw), F32),
            pltpu.VMEM((width // 2, hw), F32),
            pltpu.VMEM((width, hw), F32),
            pltpu.VMEM((hw, hw), F32),
            pltpu.VMEM((nrows, hw // 2, hw), F32),
            pltpu.VMEM((hw // 2, hw), F32),
            pltpu.VMEM((hw, hw), F32),
            pltpu.VMEM((tiles, wide, tile), BF16),
            pltpu.VMEM((tiles, wide, tile), BF16),
            pltpu.VMEM((tiles, width, tile), BF16),
            pltpu.VMEM((tiles, width, tile), BF16),
            dma((nh + 2,)),
            dma((1,)), dma((nh, lines)), dma((nh, lines // 2)),
            dma((1,)), dma((nh,)), dma((nh, nrows * group)), dma((nh,)),
            dma((1,)), dma((nh, nrows // 2)),
            dma((1,)), dma((nh,)), dma((1,)), dma((nh, 3)), dma((1,)),
        ],
        compiler_params=pltpu.CompilerParams(
            collective_id=0, has_side_effects=True, vmem_limit_bytes=limit),
    )(*(pltpu.with_memory_space_constraint(v, pltpu.HBM) for v in (matrix, panel, factor)))
    return pl.pallas_call(
        functools.partial(hand_out, tile),
        out_shape=(jax.ShapeDtypeStruct(matrix.shape, F32), jax.ShapeDtypeStruct(panel.shape, F32)),
        in_specs=[vmem] * 6,
        out_specs=(hbm, hbm),
        scratch_shapes=[pltpu.VMEM((total, wide), F32), dma((tiles + 1,))],
        compiler_params=pltpu.CompilerParams(vmem_limit_bytes=8 * total * wide * 4 + (4 << 20)),
    )(*held)


def solution(mesh):
    in_specs = (P("row", "col"), P(("row", "col"), None), P())
    out_specs = (P("row", "col"), P(("row", "col"), None))
    return jax.shard_map(
        functools.partial(per_device, mesh.shape["row"], mesh.shape["col"]),
        mesh=mesh, in_specs=in_specs, out_specs=out_specs, check_vma=False)
```

```python
import functools

import jax
import jax.numpy as jnp
from jax import lax
from jax.experimental import pallas as pl
from jax.experimental.pallas import tpu as pltpu
from jax.sharding import PartitionSpec as P

F32 = jnp.float32
BF16 = jnp.bfloat16
NN = (((1,), (0,)), ((), ()))
NT = (((1,), (1,)), ((), ()))


def split(x):
    high = x.astype(BF16)
    return high, (x - high.astype(F32)).astype(BF16)


def mult(a, b, dims=NN):
    dot = functools.partial(lax.dot_general, dimension_numbers=dims, preferred_element_type=F32)
    return dot(a[0], b[1]) + dot(a[1], b[0]) + dot(a[0], b[0])


def wide_of(ref, span):
    return jnp.concatenate([ref[0, span, :], ref[1, span, :]], axis=1)


def tile_loop(count, body):
    if count <= 2:
        for i in range(count):
            body(i)
    else:
        pl.loop(0, count)(body)


def kernel(nrows, ncols, tile, a_hbm, panel_hbm, t_hbm, out_ref, corr_ref, v_hi, v_lo, y_hi, y_lo,
           a_ref, t_ref, vr, vc, sr, sc, q, qin, kpart, kin, kpair, kside, kfull,
           lpart, lin, lpair, lfull,
           at_hi, at_lo, vt_hi, vt_lo,
           local_sem, v_send, v_recv, vf_recv, q_send, q_recv, s_recv, sf_recv, sc_send, sc_recv,
           vc_send, vc_recv, k_send, k_recv, kg_recv):
    r, c = lax.axis_index("row"), lax.axis_index("col")
    lines = ncols // 2
    group = ncols // (2 * nrows)
    z, y = c // 2, c % 2
    total = a_ref.shape[0]
    nh, wide, hw = sc.shape
    blk, width = panel_hbm.shape
    tiles = total // tile
    mate = r + 1 - 2 * (r % 2)

    def rows(index, size):
        return pl.ds(pl.multiple_of(index * size, size), size)

    def peer(d):
        line = z
        for b in range(lines.bit_length()):
            if d >> b & 1:
                line = line + (1 << b) - (2 << b) * (z // (1 << b) % 2)
        return line

    def copy(src, dst, send, recv, row, col):
        return pltpu.make_async_remote_copy(
            src_ref=src, dst_ref=dst, send_sem=send, recv_sem=recv,
            device_id=(row, col), device_id_type=pl.DeviceIdType.MESH)

    def go(desc, when=None):
        if when is None:
            desc.start()
        else:
            pl.when(when)(desc.start)

    def sent(ref, sem):
        copy(ref, ref, sem, kg_recv.at[0], r, c).wait_send()

    def landed(ref, sem):
        copy(ref, ref, k_send.at[0], sem, r, c).wait_recv()

    def some(ref, h, count):
        return ref.at[h, pl.ds(0, count * blk), :]

    loads = [pltpu.make_async_copy(panel_hbm.at[:, pl.ds(h * hw, hw)], vr.at[h, rows(c, blk), :], local_sem.at[0])
             for h in range(nh)]
    loads.append(pltpu.make_async_copy(a_hbm, a_ref, local_sem.at[1]))
    loads.append(pltpu.make_async_copy(t_hbm, t_ref, local_sem.at[2]))
    for load in loads[:nh]:
        load.start()

    across = z * 2 + 1 - y
    target = z // group
    barrier = pltpu.get_barrier_semaphore()

    def greet(row, col):
        pl.semaphore_signal(barrier, inc=1, device_id=(row, col), device_id_type=pl.DeviceIdType.MESH)

    for d in reversed(range(1, lines)):
        greet(r, peer(d) * 2 + y)
    greet(r, across)
    for d in range(1, nrows):
        greet(lax.rem(r + d, nrows), c)
    for load in loads[nh:]:
        load.start()
    both = vr.at[:, rows(c, blk), :]
    pltpu.make_async_copy(both, both, local_sem.at[0]).wait()
    pl.semaphore_wait(barrier, lines + nrows - 1)

    order = list(range(1, lines))
    for h in range(nh):
        own = vr.at[h, rows(c, blk), :]
        go(copy(own, own, v_send.at[0], v_recv.at[h, z], r, across))
        for d in order:
            go(copy(own, own, v_send.at[0], v_recv.at[h, z], r, peer(d) * 2 + y))

    loads[nh].wait()

    def flip(i):
        high, low = split(a_ref[pl.ds(pl.multiple_of(i * tile, tile), tile), :].T)
        at_hi[i] = high
        at_lo[i] = low
    tile_loop(tiles, flip)
    loads[nh + 1].wait()
    t_two = split(t_ref[...])
    tt_two = split(t_ref[...].T)

    for h in range(nh):
        for d in range(1, lines):
            line = peer(d)
            slot = vr.at[h, rows(line * 2 + y, blk), :]
            landed(slot, v_recv.at[h, line])
            go(copy(slot, slot, v_send.at[0], vf_recv.at[h, d // 2], r, across))

    holder = c * nrows // ncols
    first_block = lax.rem(c * nrows, ncols)
    same = r % 2 == holder % 2

    def hand_panel(h):
        held = vr.at[h, rows(first_block // nrows, wide), :]
        kept = vc.at[h]
        for d in range(1, nrows // 2):
            go(copy(held, kept, vc_send.at[0], vc_recv.at[h], lax.rem(r + 2 * d, nrows), c), r == holder)
        go(copy(held, kept, vc_send.at[0], vc_recv.at[h], mate, c), r == holder)

        @pl.when(r == holder)
        def _():
            kept[...] = held[...]

    def pass_panel(h):
        kept = vc.at[h]

        @pl.when((r != holder) & same)
        def _():
            landed(kept, vc_recv.at[h])
            copy(kept, kept, vc_send.at[0], vc_recv.at[h], mate, c).start()

    def take_panel(h):
        pl.when(jnp.logical_not(same))(functools.partial(landed, vc.at[h], vc_recv.at[h]))

    def reduce_product(h):
        for e in range(tiles):
            if e == 0:
                landed(some(vr, h, 1), v_recv.at[h, z])
            landed(some(vr, h, 2 if e else 1), vf_recv.at[h, e])
            i = peer(2 * e) // 2
            part = mult((at_hi[i], at_lo[i]), split(vr[h, rows(i, tile), :]))
            q[h] = part if e == 0 else q[h] + part
        for d in range(1, nrows):
            other = lax.rem(r + d, nrows)
            go(copy(q.at[h, rows(other, blk), :], qin.at[h, d], q_send.at[0], q_recv.at[h], other, c))

    reduce_product(0)
    hand_panel(0)
    reduce_product(1)

    def turn(i):
        span = pl.ds(pl.multiple_of(i * tile, tile), tile)
        v_two = split(wide_of(vr, span))
        v_hi[span, :], v_lo[span, :] = v_two
        high, low = split(mult(tt_two, v_two, NT))
        vt_hi[i] = high
        vt_lo[i] = low

    place = lax.rem(c * nrows + r, ncols)
    here = r * group + lax.rem(z, group)
    products = []
    for h in range(nh):
        landed(qin.at[h, pl.ds(1, nrows - 1)], q_recv.at[h])
        product = q[h, rows(r, blk), :]
        for d in range(1, nrows):
            product = product + qin[h, d]
        products.append(split(product))
        scaled = None
        for g in range(h + 1):
            block = tuple(t[g * hw:(g + 1) * hw, h * hw:(h + 1) * hw] for t in t_two)
            term = mult(products[g], block)
            scaled = term if scaled is None else scaled + term
        mine = sc.at[h, rows(r, blk), :]
        mine[...] = scaled
        slot = sr.at[h, rows(place, blk), :]
        for d in [1] + order[:0:-1]:
            go(copy(mine, slot, q_send.at[0], s_recv.at[h, here], target, peer(d) * 2 + y))
        for d in range(1, nrows // 2):
            go(copy(mine, mine, sc_send.at[0], sc_recv.at[h, d], lax.rem(r + 2 * d, nrows), c))
        go(copy(mine, mine, sc_send.at[0], sc_recv.at[h, 0], mate, c))
        if h == 0:
            hand_panel(1)
            tile_loop(tiles, turn)

    def from_mate(h):
        landed(some(sc, h, nrows // 2), sc_recv.at[h, 0])

    def hand_on(h):
        for d in range(1, nrows // 2):
            slot = sc.at[h, rows(lax.rem(r - 2 * d + nrows, nrows), blk), :]
            landed(slot, sc_recv.at[h, d])
            go(copy(slot, slot, sc_send.at[0], sc_recv.at[h, 0], mate, c))

    def forward_scaled(h):
        pl.when(target // 2 == r // 2)(functools.partial(hand_on, h))
        pl.when(target == r)(functools.partial(from_mate, h))
        for g in range(group):
            line = r * group + g
            for d in range(nrows):
                j = lax.rem((mate if d % 2 else r) + d // 2 * 2, nrows)
                at = j * group + g
                slot = sr.at[h, rows(lax.rem((line * 2 + y) * nrows + j, ncols), blk), :]
                held = sc.at[h, rows(j, blk), :]
                straight = copy(held, slot, sc_send.at[0], sf_recv.at[h], r, across)
                passed = copy(slot, slot, sc_send.at[0], sf_recv.at[h], r, across)

                @pl.when(z == line)
                def _():
                    straight.start()
                    slot[...] = held[...]

                @pl.when(z != line)
                def _():
                    landed(slot, s_recv.at[h, at])
                    passed.start()


    def gather_scaled(h):
        landed(some(sr, h, nrows * group), sf_recv.at[h])

    def small(h, part, base):
        part[...] = jnp.zeros_like(part)
        for g in range(group):
            start = lax.rem(((r * group + g) * 2 + y) * nrows, ncols) * blk // tile
            for i in range(nrows * blk // tile):
                at = start + i
                part[...] += mult((vt_hi[at, base:, :], vt_lo[at, base:, :]), split(sr[h, rows(at, tile), :]))

    def pair_up(h, part, room, pair):
        size = pair.shape[0]
        go(copy(part.at[rows(mate % 2, size), :], room.at[0], k_send.at[0], k_recv.at[3 * h], mate, c))
        landed(room.at[0], k_recv.at[3 * h])
        pair[...] = part[rows(r % 2, size), :] + room[0]

    def spread(h, step, room, pair, slots):
        for i in slots:
            row, col = lax.rem(r + i // 2 * 2, nrows), across if i % 2 else c
            go(copy(pair, room.at[i], k_send.at[0], k_recv.at[3 * h + step], row, col))

    def collect(h, step, room, pair, slots):
        landed(room.at[pl.ds(0, len(slots))], k_recv.at[3 * h + step])
        summed = pair[...]
        for i in slots:
            summed = summed + room[i]
        return summed

    def finish_half(h, full, summed):
        mine = full.at[rows(r % 2, summed.shape[0]), :]
        mine[...] = summed
        go(copy(mine, mine, k_send.at[0], kg_recv.at[0], mate, c))


    forward_scaled(0)
    small(0, kpart, 0)
    pair_up(0, kpart, kin, kpair)
    spread(0, 1, kin, kpair, range(2, nrows, 2))
    forward_scaled(1)
    small(1, lpart, hw)
    pair_up(1, lpart, lin, lpair)
    spread(1, 1, lin, lpair, range(1, nrows))
    for h in range(nh):
        pl.when(target // 2 != r // 2)(functools.partial(hand_on, h))
    pass_panel(0)
    pass_panel(1)
    sent(vr.at[:, pl.ds(0, (2 * lines - 1) * blk), :], v_send.at[0])
    sent(sr.at[:, pl.ds(0, (nrows + lines - 2) * blk), :], q_send.at[0])
    kside[...] = collect(0, 1, kin, kpair, range(2, nrows, 2))
    spread(0, 2, kin, kside, (1,))
    gather_scaled(0)
    take_panel(0)
    take_panel(1)
    for h in range(nh):
        pl.when(target != r)(functools.partial(from_mate, h))
    everything = pl.ds(0, wide)
    sc_turned = wide_of(sc, everything).T
    vc_turned = split(wide_of(vc, everything).T)
    vc_near, vc_rest = (tuple(v[h * hw:(h + 1) * hw, :] for v in vc_turned) for h in range(nh))

    def first(i):
        span = pl.ds(pl.multiple_of(i * tile, tile), tile)
        out_ref[span, :] = a_ref[span, :] - mult(split(sr[0, span, :]), vc_near)
    tile_loop(tiles, first)

    def second(i):
        span = pl.ds(pl.multiple_of(i * tile, tile), tile)
        out_ref[span, :] = out_ref[span, :] - mult(split(sr[1, span, :]), vc_rest)
    finish_half(1, lfull, collect(1, 1, lin, lpair, range(1, nrows)))
    finish_half(0, kfull, collect(0, 2, kin, kside, (1,)))
    gather_scaled(1)
    tile_loop(tiles, second)
    landed(vr.at[0, pl.ds(0, kpair.shape[0] + lpair.shape[0]), :], kg_recv.at[0])
    left = kfull[...]
    right = jnp.concatenate([left[hw:, :].T, lfull[...]], axis=0)
    k_two = split(jnp.concatenate([left, right], axis=1))
    y_hi[...], y_lo[...] = split(sc_turned - mult(k_two, vc_turned))
    mine = rows(c, blk)
    corr_ref[...] = wide_of(sr, mine) - 0.5 * mult((v_hi[mine, :], v_lo[mine, :]), k_two)
    sent(sr.at[:, pl.ds(0, (nrows - 1 + nrows * group) * blk), :], sc_send.at[0])

    @pl.when(r == holder)
    def _():
        sent(vr.at[:, pl.ds(0, nrows // 2 * wide), :], vc_send.at[0])

    @pl.when((r != holder) & same)
    def _():
        sent(vc, vc_send.at[0])
    moved = (nrows // 2 + 2) * kpair.shape[0] + (nrows + 1) * lpair.shape[0]
    sent(vr.at[:, pl.ds(0, moved // nh), :], k_send.at[0])


def hand_out(tile, held_ref, held_corr_ref, v_hi, v_lo, y_hi, y_lo, out_hbm, corr_hbm, stage, sem):
    tiles = held_ref.shape[0] // tile
    copies = [pltpu.make_async_copy(held_corr_ref, corr_hbm, sem.at[tiles])]
    copies[0].start()
    for i in range(tiles):
        span = pl.ds(i * tile, tile)
        stage[span, :] = held_ref[span, :] - mult((v_hi[span, :], v_lo[span, :]), (y_hi[...], y_lo[...]))
        copies.append(pltpu.make_async_copy(stage.at[span, :], out_hbm.at[span, :], sem.at[i]))
        copies[-1].start()
    for copy in copies:
        copy.wait()


def per_device(nrows, ncols, matrix, panel, factor):
    total, wide = matrix.shape
    blk, width = panel.shape
    tile = 4 * blk
    tiles = total // tile
    group = ncols // (2 * nrows)
    lines = ncols // 2
    nh = 2
    hw = width // nh
    dma = pltpu.SemaphoreType.DMA
    vmem = pl.BlockSpec(memory_space=pltpu.VMEM)
    hbm = pl.BlockSpec(memory_space=pltpu.HBM)
    limit = 4 * (5 * total * wide + 4 * total * width + 4 * wide * width + 16 * width * width) + (8 << 20)
    held = pl.pallas_call(
        functools.partial(kernel, nrows, ncols, tile),
        out_shape=(jax.ShapeDtypeStruct(matrix.shape, F32), jax.ShapeDtypeStruct(panel.shape, F32),
                   jax.ShapeDtypeStruct((total, width), BF16), jax.ShapeDtypeStruct((total, width), BF16),
                   jax.ShapeDtypeStruct((width, wide), BF16), jax.ShapeDtypeStruct((width, wide), BF16)),
        in_specs=[hbm] * 3,
        out_specs=(vmem,) * 6,
        scratch_shapes=[
            pltpu.VMEM((total, wide), F32),
            pltpu.VMEM((width, width), F32),
            pltpu.VMEM((nh, total, hw), F32),
            pltpu.VMEM((nh, wide, hw), F32),
            pltpu.VMEM((nh, total, hw), F32),
            pltpu.VMEM((nh, wide, hw), F32),
            pltpu.VMEM((nh, wide, hw), F32),
            pltpu.VMEM((nh, nrows, blk, hw), F32),
            pltpu.VMEM((width, hw), F32),
            pltpu.VMEM((nrows, width // 2, hw), F32),
            pltpu.VMEM((width // 2, hw), F32),
            pltpu.VMEM((width // 2, hw), F32),
            pltpu.VMEM((width, hw), F32),
            pltpu.VMEM((hw, hw), F32),
            pltpu.VMEM((nrows, hw // 2, hw), F32),
            pltpu.VMEM((hw // 2, hw), F32),
            pltpu.VMEM((hw, hw), F32),
            pltpu.VMEM((tiles, wide, tile), BF16),
            pltpu.VMEM((tiles, wide, tile), BF16),
            pltpu.VMEM((tiles, width, tile), BF16),
            pltpu.VMEM((tiles, width, tile), BF16),
            dma((3,)),
            dma((1,)), dma((nh, lines)), dma((nh, lines // 2)),
            dma((1,)), dma((nh,)), dma((nh, nrows * group)), dma((nh,)),
            dma((1,)), dma((nh, nrows // 2)),
            dma((1,)), dma((nh,)), dma((1,)), dma((3 * nh - 1,)), dma((1,)),
        ],
        compiler_params=pltpu.CompilerParams(
            collective_id=0, has_side_effects=True, vmem_limit_bytes=limit),
    )(*(pltpu.with_memory_space_constraint(v, pltpu.HBM) for v in (matrix, panel, factor)))
    return pl.pallas_call(
        functools.partial(hand_out, tile),
        out_shape=(jax.ShapeDtypeStruct(matrix.shape, F32), jax.ShapeDtypeStruct(panel.shape, F32)),
        in_specs=[vmem] * 6,
        out_specs=(hbm, hbm),
        scratch_shapes=[pltpu.VMEM((total, wide), F32), dma((tiles + 1,))],
        compiler_params=pltpu.CompilerParams(vmem_limit_bytes=8 * total * wide * 4 + (4 << 20)),
    )(*held)


def solution(mesh):
    in_specs = (P("row", "col"), P(("row", "col"), None), P())
    out_specs = (P("row", "col"), P(("row", "col"), None))
    return jax.shard_map(
        functools.partial(per_device, mesh.shape["row"], mesh.shape["col"]),
        mesh=mesh, in_specs=in_specs, out_specs=out_specs, check_vma=False)
```
